32 devices in a mesh: member: 8 (over y, x, core), band: 4 (over z).
Axes of the slice: x: 2, y: 2, z: 4, core: 2. Of those that a mesh axis runs over, the one named last changes fastest.
Arguments:
- height_start: float32 [80, 256, 512], P(None, 'member', 'band'), may hold values from -6 to 6
- east_start: float32 [80, 256, 512], P(None, 'member', 'band'), may hold values from -6 to 6
- north_start: float32 [80, 256, 512], P(None, 'member', 'band'), may hold values from -6 to 6
- obs_value: float32 [256, 512], P('member', 'band'), may hold values from -8 to 8
- obs_mask: int32 [256, 512], P('member', 'band'), may hold values 0 or 1
- obs_precision: float32 [256, 512], P('member', 'band'), may hold values from 0.25 to 4
- step_sizes: int32 [2], replicated, may hold values from 4 to 12
Outputs:
- analysis_height: float32 [80, 256, 512], P(None, 'member', 'band')
- analysis_east: float32 [80, 256, 512], P(None, 'member', 'band')
- analysis_north: float32 [80, 256, 512], P(None, 'member', 'band')
The draws below stay inside these ranges and needn't reach their ends.
All inputs are finite; a program needn't handle non-finite values. No bound on the sum of `obs_mask` on one device may be relied on, other than what follows from the above.
Results may differ from the reference program's by a relative error of at most 0.0001.
Values sent between devices are 32-bit elements; how exact they have to be, the bound alone decides.
No kernel may reach another device: no remote copies, remote signals or barrier semaphores. Data moves between devices by JAX's collectives and lax.ppermute only.
A program may use at most 128 MiB of HBM per device.

```python
import math
import jax
import jax.numpy as jnp
from jax import lax

MEMBERS = 80
STEPS = 3
ITERS = 2
LWIDTH = 32
LSCALE = 12
LAT = 256
LON = 512


def with_ends(values, stream_key, least, largest):
    dims = values.shape
    spot = [jax.random.randint(jax.random.fold_in(stream_key, axis), (), 0, dims[axis]) for axis in range(len(dims))]
    values = values.at[tuple(spot)].set(least)
    longest = dims.index(max(dims))
    spot[longest] = (spot[longest] + 1) % dims[longest]
    return values.at[tuple(spot)].set(largest)


def block_scale(rng, shape, pieces, smallest, top_value):
    loudness, own = 1.0, jax.random.fold_in(rng, 6)
    for position, shards_of in pieces:
        heights = jnp.exp(jax.random.uniform(jax.random.fold_in(own, position), (shards_of,), jnp.float32, smallest / len(pieces), top_value / len(pieces)))
        loudness = loudness * jnp.repeat(heights, shape[position] // shards_of).reshape([-1 if axis == position else 1 for axis in range(len(shape))])
    return loudness


def normal_values(rng, extent, scale, limit, pieces=(), kind=jnp.bfloat16):
    loudness = block_scale(rng, extent, pieces, -0.22, 0.18) if pieces else 1.0
    values = jax.random.normal(rng, extent, jnp.float32) * scale * loudness
    return jnp.minimum(jnp.maximum(values, -limit), limit).astype(kind)


def setup_inputs(seed: int = 0) -> dict:
    seeds = jax.random.split(jax.random.key(seed), 8)
    height_start = normal_values(seeds[0], (MEMBERS, LAT, LON), 1.0, 6.0, ((1, 8), (2, 4)), jnp.float32)
    east_start = normal_values(seeds[1], (MEMBERS, LAT, LON), 1.0, 6.0, ((1, 8), (2, 4)), jnp.float32)
    north_start = normal_values(seeds[2], (MEMBERS, LAT, LON), 1.0, 6.0, ((1, 8), (2, 4)), jnp.float32)
    obs_value = normal_values(seeds[3], (LAT, LON), 1.5, 8.0, ((0, 8), (1, 4)), jnp.float32)
    obs_mask = with_ends((jax.random.randint(seeds[4], (LAT, LON), 0, 2) < 1).astype(jnp.int32), jax.random.fold_in(seeds[4], 1), 0, 1)
    obs_precision = jnp.clip(jnp.exp(math.log(4.0) - 2.7725887 * jax.random.uniform(seeds[5], (LAT, LON), jnp.float32) ** block_scale(seeds[5], (LAT, LON), ((0, 8), (1, 4)), -0.2, 0.2)), 0.25, 4.0)
    step_sizes = jax.random.randint(seeds[6], (ITERS,), 4, 13).astype(jnp.int32)
    return {"height_start": height_start, "east_start": east_start, "north_start": north_start, "obs_value": obs_value, "obs_mask": obs_mask, "obs_precision": obs_precision, "step_sizes": step_sizes}


highest = lax.Precision.HIGHEST

def taper_kernel(outputs, inputs, margin, spread):
    out_index = jnp.arange(outputs, dtype=jnp.int32)[:, None]
    in_index = jnp.arange(inputs, dtype=jnp.int32)[None, :]
    offset = (in_index - margin - out_index).astype(jnp.float32)
    scaled_off = offset / spread
    weight = jnp.exp(-0.5 * scaled_off * scaled_off)
    return jnp.where(jnp.abs(offset) <= margin, weight, jnp.zeros_like(weight))

def taper_rows(padded, row_count, margin, spread):
    kernel = taper_kernel(row_count, row_count + 2 * margin, margin, spread)
    return jnp.einsum('ab,mbc->mac', kernel, padded, precision=highest)

def taper_columns(padded, columns, margin, spread):
    block_size = 128 if columns % 128 == 0 else columns
    windows = jnp.stack([lax.slice_in_dim(padded, block_start, block_start + block_size + 2 * margin, axis=2) for block_start in range(0, columns, block_size)], axis=2)
    kernel = taper_kernel(block_size, block_size + 2 * margin, margin, spread)
    result = jnp.einsum('mrjk,bk->mrjb', windows, kernel, precision=highest)
    return result.reshape(padded.shape[0], padded.shape[1], columns)

def lon_diff(grid_field):
    return jnp.roll(grid_field, -1, axis=2) - jnp.roll(grid_field, 1, axis=2)

def lat_diff(grid_field):
    padded = jnp.pad(grid_field, ((0, 0), (1, 1), (0, 0)))
    return padded[:, 2:, :] - padded[:, :-2, :]

def advance(height, eastward, northward):
    new_height = height - 0.2 * (lon_diff(eastward) + lat_diff(northward))
    new_east = eastward + 0.1 * northward - 0.2 * lon_diff(new_height)
    new_north = northward - 0.1 * eastward - 0.2 * lat_diff(new_height)
    return (new_height, new_east, new_north)

def localize(contrib):
    margin = LWIDTH
    padded = jnp.pad(contrib, ((0, 0), (margin, margin), (0, 0)))
    lat_done = taper_rows(padded, contrib.shape[1], margin, LSCALE)
    wrapped = jnp.concatenate([lat_done[:, :, -margin:], lat_done, lat_done[:, :, :margin]], axis=2)
    return taper_columns(wrapped, contrib.shape[2], margin, LSCALE)

def member_sum(anomaly, weights):
    return lax.optimization_barrier(jnp.sum(anomaly * weights, axis=0))

def reference(height_start, east_start, north_start, obs_value, obs_mask, obs_precision, step_sizes):
    height, eastward, northward = (height_start, east_start, north_start)
    for section_number in range(STEPS):
        height, eastward, northward = advance(height, eastward, northward)
    members = height.shape[0]
    root_scale = jnp.sqrt(jnp.float32(members - 1))
    mean_height = lax.optimization_barrier(jnp.sum(height, axis=0)) / members
    mean_east = lax.optimization_barrier(jnp.sum(eastward, axis=0)) / members
    mean_north = lax.optimization_barrier(jnp.sum(northward, axis=0)) / members
    anom_height = (height - mean_height) / root_scale
    anom_east = (eastward - mean_east) / root_scale
    anom_north = (northward - mean_north) / root_scale
    obs_weight = obs_mask.astype(jnp.float32) * obs_precision
    weights = jnp.zeros_like(height)
    cell_total = float(members * height.shape[1] * height.shape[2])
    for iteration in range(ITERS):
        state_height = mean_height + member_sum(anom_height, weights)
        state_east = mean_east + member_sum(anom_east, weights)
        state_north = mean_north + member_sum(anom_north, weights)
        residual = obs_weight * (obs_value - state_height - 0.15 * (state_east * state_east + state_north * state_north))
        contrib = (anom_height + 0.3 * (state_east * anom_east + state_north * anom_north)) * residual
        gradient = weights - localize(contrib)
        square_total = jnp.sum(gradient * gradient)
        factor = step_sizes[iteration].astype(jnp.float32) / 64.0 / jnp.sqrt(square_total / cell_total + 1e-06)
        weights = weights - factor * gradient
    return (height + member_sum(anom_height, weights), eastward + member_sum(anom_east, weights), northward + member_sum(anom_north, weights))
```

```python
import functools

import jax
import jax.numpy as jnp
import numpy as np
from jax import lax
from jax.experimental import pallas as pl
from jax.experimental.pallas import tpu as pltpu
from jax.sharding import PartitionSpec as P

STEPS = 3
ITERS = 2
LWIDTH = 32
LSCALE = 12

LANES = 128
SUB = 8
SLOT = 16
EAST, SIDE = 2 * STEPS, 2 * STEPS - 1
PACK = LANES // SLOT
FOLD = LANES // LWIDTH

VMEM = pl.BlockSpec(memory_space=pltpu.VMEM)
SMEM = pl.BlockSpec(memory_space=pltpu.SMEM)


def f32(*shape):
    return jax.ShapeDtypeStruct(shape, jnp.float32)


def iota(shape, axis):
    return lax.broadcasted_iota(jnp.int32, shape, axis)


def spin(block, shift, axis):
    shift %= block.shape[axis]
    return block if shift == 0 else pltpu.roll(block, shift, axis)


def shifted(block, axis, step, periodic):
    count = lax.axis_size(axis)
    if periodic:
        pairs = [(i, (i + step) % count) for i in range(count)]
    else:
        pairs = [(i, i + step) for i in range(count) if 0 <= i + step < count]
    return lax.ppermute(block, axis, pairs)


def everywhere_sum(block):
    for axis in ("band", "member"):
        count = lax.axis_size(axis)
        if count & (count - 1):
            block = lax.psum(block, axis)
            continue
        reach = 1
        while reach < count:
            block = block + lax.ppermute(block, axis, [(i, i ^ reach) for i in range(count)])
            reach *= 2
    return block


def taper(offset):
    scaled = offset.astype(np.float32) / np.float32(LSCALE)
    weight = np.exp(np.float32(-0.5) * scaled * scaled)
    return np.where(np.abs(offset) <= LWIDTH, weight, np.float32(0)).astype(np.float32)


def two_terms(table):
    high = table.astype(jnp.bfloat16)
    low = (table - high.astype(np.float32)).astype(jnp.bfloat16)
    return high, low


def row_table(rows):
    out = np.arange(rows)[:, None]
    table = taper(np.arange(rows + 2 * LWIDTH)[None, :] - LWIDTH - out)
    high, low = two_terms(table)
    return np.block([[high, high], [low, np.zeros_like(low)]])


def column_table(cols):
    out = np.arange(cols)
    high, low = two_terms(taper(out[:, None] - out[None, :]))
    return np.block([[high, low], [high, np.zeros_like(low)]])


def strip_table(cols):
    near = np.arange(LWIDTH)
    left = taper((near - LWIDTH)[:, None] - near[None, :])
    right = taper((cols + near)[:, None] - (cols - LWIDTH + near)[None, :])
    table = np.zeros((2 * LANES, 2 * LANES), np.float32)
    for k in range(FOLD):
        src, dst = k * LWIDTH, 2 * k * LWIDTH
        table[src : src + LWIDTH, dst + LWIDTH : dst + 2 * LWIDTH] = left
        table[LANES + src : LANES + src + LWIDTH, dst : dst + LWIDTH] = right
    return two_terms(table)


def split(block):
    high = block.astype(jnp.bfloat16)
    low = (block - high.astype(jnp.float32)).astype(jnp.bfloat16)
    return high, low


def mm(a, b):
    return jnp.dot(a, b, preferred_element_type=jnp.float32)


def slot_pack(east, north, height, k, side):
    cols = east.shape[-1]
    lane = iota(east.shape, 1) - SLOT * k
    base = SLOT * k
    skip = (cols - EAST, cols - SIDE) if side else (0, 0)
    e = spin(east, base - skip[0], 1)
    n = spin(north, base + EAST - skip[1], 1)
    h = spin(height, base + EAST + SIDE - skip[1], 1)
    inner = jnp.where(lane < EAST, e, jnp.where(lane < EAST + SIDE, n, h))
    return jnp.where((lane >= 0) & (lane < SLOT), inner, 0.0)


def pack_kernel(h_ref, u_ref, v_ref, top_ref, bottom_ref, left_ref, right_ref):
    rows = h_ref.shape[1]
    sub = iota((SUB, LANES), 0)
    left = right = None
    for k in range(PACK):
        u, v, h = u_ref[k], v_ref[k], h_ref[k]
        uf, vf, hf = u[:SUB], v[:SUB], h[:SUB]
        top_ref[k, :SUB] = jnp.where(sub < 6, vf, spin(uf, 6, 0))
        top_ref[k, SUB:] = jnp.where(sub < 5, hf, spin(uf, 3, 0))
        ul, vl, hl = u[rows - SUB :], v[rows - SUB :], h[rows - SUB :]
        bottom_ref[k, :SUB] = jnp.where(sub < 2, spin(ul, 5, 0), vl)
        bottom_ref[k, SUB:] = jnp.where(sub < 3, spin(ul, 3, 0), hl)
        l, r = slot_pack(u, v, h, k, 0), slot_pack(u, v, h, k, 1)
        left, right = (l, r) if k == 0 else (left + l, right + r)
    left_ref[0] = left
    right_ref[0] = right


def pack_halos(height, eastward, northward):
    members, rows, cols = height.shape
    tile = pl.BlockSpec((PACK, rows, cols), lambda g: (g, 0, 0))
    edge = pl.BlockSpec((PACK, 2 * SUB, cols), lambda g: (g, 0, 0))
    strip = pl.BlockSpec((1, rows, LANES), lambda g: (g, 0, 0))
    groups = members // PACK
    return pl.pallas_call(
        pack_kernel,
        name="pack_halos",
        grid=(groups,),
        in_specs=[tile] * 3,
        out_specs=[edge, edge, strip, strip],
        out_shape=[f32(members, 2 * SUB, cols)] * 2 + [f32(groups, rows, LANES)] * 2,
    )(height, eastward, northward)


def forecast_kernel(
    h_ref, u_ref, v_ref, above_ref, below_ref, ownl_ref, ownr_ref, hall_ref, halr_ref,
    cornu_ref, cornd_ref, obs_ref, edge_ref,
    ho_ref, uo_ref, vo_ref, mean_ref, contrib_ref,
    ext_ref, wall_ref, sum_ref,
):
    members, rows, cols = h_ref.shape
    groups = members // PACK
    tall = rows + 2 * SUB
    lane = iota((tall, LANES), 1)
    slot = lane % SLOT
    row = iota((tall, LANES), 0)
    sub = iota((SUB, LANES), 0)
    outside = ((row < SUB) & (edge_ref[0] == 1)) | ((row >= rows + SUB) & (edge_ref[1] == 1))
    pull = jnp.where(outside, 0.0, 0.2)

    def dy(x):
        return spin(x, -1, 0) - spin(x, 1, 0)

    def march(h, u, v, dx):
        dh = dx(u)
        h = h - pull * (dh + dy(v))
        new_u = u + 0.1 * v - pull * dx(h)
        new_v = v - 0.1 * u - pull * dy(h)
        return h, new_u, new_v

    def flat(x):
        return spin(x, -1, 1) - spin(x, 1, 1)

    def group(g, _):
        packs = [[None, None], [None, None]]
        for k in range(PACK):
            m = g * PACK + k
            a0, a1 = above_ref[m, :SUB], above_ref[m, SUB:]
            b0, b1 = below_ref[m, :SUB], below_ref[m, SUB:]
            ua = jnp.where(sub < 5, spin(a0, 3, 0), spin(a1, 5, 0))
            ub = jnp.where(sub < 2, spin(b0, 2, 0), spin(b1, 5, 0))
            ext_ref[k, 0, :SUB] = ua
            ext_ref[k, 0, rows + SUB :] = ub
            for end, (u, v, h) in enumerate(((ua, a0, a1), (ub, b0, b1))):
                for side in (0, 1):
                    piece = slot_pack(u, v, h, k, side)
                    packs[side][end] = piece if k == 0 else packs[side][end] + piece
        own = [
            jnp.concatenate([packs[0][0], ownl_ref[g], packs[0][1]], axis=0),
            jnp.concatenate([packs[1][0], ownr_ref[g], packs[1][1]], axis=0),
        ]
        hal = [
            jnp.concatenate([cornu_ref[g], hall_ref[g], cornd_ref[g]], axis=0),
            jnp.concatenate([cornu_ref[groups + g], halr_ref[g], cornd_ref[groups + g]], axis=0),
        ]

        def fields(first, second, at, meet, length):
            out = []
            for start, size in ((0, EAST), (EAST, SIDE), (EAST + SIDE, SIDE)):
                head = spin(first, meet - size - start, 1)
                tail = spin(second, meet - start, 1)
                out.append(jnp.where(slot < meet, head, tail))
            return out

        lu, lv, lh = fields(hal[0], own[0], 2, SUB, EAST)
        ru, rv, rh = fields(own[1], hal[1], 0, EAST, EAST)
        for step in range(STEPS):
            wall_ref[2 * step] = jnp.where(slot == SUB - 1, lu, ru)
            lh, lu, lv = march(lh, lu, lv, flat)
            rh, ru, rv = march(rh, ru, rv, flat)
            wall_ref[2 * step + 1] = jnp.where(slot == SUB - 1, lh, rh)

        sums = [sum_ref[0], sum_ref[1], sum_ref[2]]
        for k in range(PACK):
            m = g * PACK + k
            u = jnp.concatenate([ext_ref[k, 0, :SUB], u_ref[m], ext_ref[k, 0, rows + SUB :]], 0)
            v = jnp.concatenate([above_ref[m, :SUB], v_ref[m], below_ref[m, :SUB]], 0)
            h = jnp.concatenate([above_ref[m, SUB:], h_ref[m], below_ref[m, SUB:]], 0)
            stage = [0]

            def dx(x):
                wall = spin(wall_ref[stage[0]], -(SLOT * k + SUB - 1), 1)
                stage[0] += 1
                ahead = jnp.where(lane == LANES - 1, wall, spin(x, -1, 1))
                behind = jnp.where(lane == 0, wall, spin(x, 1, 1))
                return ahead - behind

            for step in range(STEPS):
                h, u, v = march(h, u, v, dx)
            h, u, v = (x[SUB : rows + SUB] for x in (h, u, v))
            ho_ref[m], uo_ref[m], vo_ref[m] = h, u, v
            sums = [s + x for s, x in zip(sums, (h, u, v))]
        for i in range(3):
            sum_ref[i] = sums[i]
        return 0

    sum_ref[...] = jnp.zeros_like(sum_ref)
    lax.fori_loop(0, groups, group, 0)
    mh, mu, mv = (sum_ref[i] / members for i in range(3))
    mean_ref[0], mean_ref[1], mean_ref[2] = mh, mu, mv
    contributions(
        (ho_ref, uo_ref, vo_ref), (mh, mu, mv), (mh, mu, mv), obs_ref, contrib_ref
    )


def contributions(fields, means, states, obs_ref, contrib_ref):
    members = contrib_ref.shape[0]
    scale = 1.0 / float(np.sqrt(np.float32(members - 1)))
    mh, mu, mv = means
    sh, su, sv = states
    residual = obs_ref[1] * (obs_ref[0] - sh - 0.15 * (su * su + sv * sv))
    residual = residual * scale
    eu, ev = 0.3 * su, 0.3 * sv

    def member(m, _):
        h, u, v = (ref[m] for ref in fields)
        contrib_ref[m] = ((h - mh) + (eu * (u - mu) + ev * (v - mv))) * residual
        return 0

    lax.fori_loop(0, members, member, 0, unroll=4)


def forecast(h, u, v, above, below, ownl, ownr, hall, halr, cornu, cornd, obs, edge):
    members, rows, cols = h.shape
    tall = rows + 2 * SUB
    return pl.pallas_call(
        forecast_kernel,
        name="forecast",
        in_specs=[VMEM] * 12 + [SMEM],
        out_specs=[VMEM] * 5,
        out_shape=[f32(members, rows, cols)] * 3 + [f32(3, rows, cols), f32(members, rows, cols)],
        scratch_shapes=[
            pltpu.VMEM((PACK, 1, tall, LANES), jnp.float32),
            pltpu.VMEM((2 * STEPS, tall, LANES), jnp.float32),
            pltpu.VMEM((3, rows, cols), jnp.float32),
        ],
    )(h, u, v, above, below, ownl, ownr, hall, halr, cornu, cornd, obs, edge)


def rows_kernel(x_ref, above_ref, below_ref, table_ref, out_ref, left_ref, right_ref):
    members, rows, cols = x_ref.shape
    lane = iota((rows, LANES), 1)
    table = table_ref[...]

    def fold(g, _):
        left = right = None
        for pair in range(FOLD // 2):
            halves = []
            for k in (2 * pair, 2 * pair + 1):
                m = g * FOLD + k
                high, low = split(jnp.concatenate([above_ref[m], x_ref[m], below_ref[m]], axis=0))
                halves.append(jnp.concatenate([high, low], axis=0))
            both = mm(table, jnp.concatenate(halves, axis=1))
            both = both[:rows] + both[rows:]
            for k in (2 * pair, 2 * pair + 1):
                y = both[:, (k % 2) * cols : (k % 2 + 1) * cols]
                out_ref[g * FOLD + k] = y
                here = lane // LWIDTH == k
                l = jnp.where(here, spin(y, LWIDTH * k, 1), 0.0)
                r = jnp.where(here, spin(y, LWIDTH * k + LWIDTH - cols, 1), 0.0)
                left, right = (l, r) if k == 0 else (left + l, right + r)
        left_ref[g] = left
        right_ref[g] = right
        return 0

    lax.fori_loop(0, members // FOLD, fold, 0)


def taper_rows(x, above, below):
    members, rows, cols = x.shape
    folds = members // FOLD
    return pl.pallas_call(
        rows_kernel,
        name="taper_rows",
        in_specs=[VMEM] * 4,
        out_specs=[VMEM] * 3,
        out_shape=[f32(members, rows, cols)] + [f32(folds, rows, LANES)] * 2,
    )(x, above, below, row_table(rows))


def columns_kernel(
    first, x_ref, left_ref, right_ref, h_ref, u_ref, v_ref, mean_ref, *refs
):
    if first:
        table_ref, high_ref, low_ref, grad_ref, sums_ref, square_ref = refs
    else:
        prev_ref, factor_ref, table_ref, high_ref, low_ref, sums_ref, square_ref = refs
    members, rows, cols = x_ref.shape
    scale = 1.0 / float(np.sqrt(np.float32(members - 1)))
    lane = iota((rows, LANES), 1)
    rim = (lane < LWIDTH) | (lane >= cols - LWIDTH)
    table, high_table, low_table = table_ref[...], high_ref[...], low_ref[...]
    means = [mean_ref[i] for i in range(3)]
    fields = (h_ref, u_ref, v_ref)

    def fold(g, carry):
        sums, square = carry
        xh, xl = split(jnp.concatenate([left_ref[g], right_ref[g]], axis=1))
        strips = mm(xh, high_table) + (mm(xl, high_table) + mm(xh, low_table))
        block = jnp.concatenate([x_ref[g * FOLD + k] for k in range(FOLD)], axis=0)
        bh, bl = split(block)
        both = mm(jnp.concatenate([bh, bl], axis=1), table)
        both = both[:, :cols] + both[:, cols:]
        for k in range(FOLD):
            m = g * FOLD + k
            at = 2 * k * LWIDTH
            part = strips[:, at // LANES * LANES : at // LANES * LANES + LANES]
            part = spin(part, -(at % LANES + LWIDTH), 1)
            y = both[k * rows : (k + 1) * rows] + jnp.where(rim, part, 0.0)
            if first:
                grad_ref[m] = y
            else:
                y = factor_ref[0] * prev_ref[m] - y
            square = square + y * y
            sums = [s + (ref[m] - mean) * y for s, ref, mean in zip(sums, fields, means)]
        return sums, square

    zero = jnp.zeros((rows, cols), jnp.float32)
    sums, square = lax.fori_loop(0, members // FOLD, fold, ([zero] * 3, zero))
    for i in range(3):
        sums_ref[i] = sums[i] * scale
    total = square[:SUB]
    for start in range(SUB, rows, SUB):
        total = total + square[start : start + SUB]
    square_ref[...] = total


def taper_columns(x, left, right, fields, means, prev=None, factor=None):
    members, rows, cols = x.shape
    first = prev is None
    high, low = strip_table(cols)
    operands = [x, left, right, *fields, means]
    specs = [VMEM] * 7
    if not first:
        operands += [prev, factor]
        specs += [VMEM, SMEM]
    operands += [column_table(cols), high, low]
    specs += [VMEM] * 3
    outs = [f32(3, rows, cols), f32(SUB, LANES)]
    if first:
        outs = [f32(members, rows, cols)] + outs
    return pl.pallas_call(
        functools.partial(columns_kernel, first),
        name="taper_columns",
        in_specs=specs,
        out_specs=[VMEM] * len(outs),
        out_shape=outs,
    )(*operands)


def contrib_kernel(h_ref, u_ref, v_ref, mean_ref, sums_ref, obs_ref, factor_ref, contrib_ref):
    means = [mean_ref[i] for i in range(3)]
    states = [mean_ref[i] + factor_ref[0] * sums_ref[i] for i in range(3)]
    contributions((h_ref, u_ref, v_ref), means, states, obs_ref, contrib_ref)


def second_contributions(fields, means, sums, obs, factor):
    return pl.pallas_call(
        contrib_kernel,
        name="second_contributions",
        in_specs=[VMEM] * 6 + [SMEM],
        out_specs=VMEM,
        out_shape=f32(*fields[0].shape),
    )(*fields, means, sums, obs, factor)


def per_device(
    height_start, east_start, north_start, obs_value, obs_mask, obs_precision, step_sizes
):
    members, rows, cols = height_start.shape
    top, bottom, ownl, ownr = pack_halos(height_start, east_start, north_start)
    hall = shifted(ownr, "band", 1, True)
    halr = shifted(ownl, "band", -1, True)
    above = shifted(bottom, "member", 1, False)
    below = shifted(top, "member", -1, False)
    ends = jnp.concatenate([hall, halr], axis=0)
    cornu = shifted(ends[:, rows - SUB :], "member", 1, False)
    cornd = shifted(ends[:, :SUB], "member", -1, False)

    obs = jnp.stack([obs_value, obs_mask.astype(jnp.float32) * obs_precision])
    here = lax.axis_index("member")
    edge = jnp.stack([here == 0, here == lax.axis_size("member") - 1]).astype(jnp.int32)
    h, u, v, means, contrib = forecast(
        height_start, east_start, north_start, above, below, ownl, ownr, hall, halr,
        cornu, cornd, obs, edge,
    )
    fields = (h, u, v)
    cells = float(members * rows * cols * lax.axis_size("member") * lax.axis_size("band"))

    def localized(contrib, *more):
        above = shifted(contrib, "member", 1, False)
        below = shifted(contrib, "member", -1, False)
        x, first, last = taper_rows(contrib, above, below)
        left = shifted(last, "band", 1, True)
        right = shifted(first, "band", -1, True)
        return taper_columns(x, left, right, fields, means, *more)

    def factor_of(square, k):
        total = jnp.sum(everywhere_sum(square))
        return step_sizes[k].astype(jnp.float32) / 64.0 / jnp.sqrt(total / cells + 1e-06)

    smooth, sums0, square = localized(contrib)
    f0 = factor_of(square, 0)
    contrib = second_contributions(fields, means, sums0, obs, f0[None])
    sums1, square = localized(contrib, smooth, f0[None])
    f1 = factor_of(square, 1)
    increment = f0 * sums0 - f1 * sums1
    return tuple(field + increment[i] for i, field in enumerate(fields))


def solution(mesh):
    tile, flat = P(None, "member", "band"), P("member", "band")
    return jax.shard_map(
        per_device,
        mesh=mesh,
        in_specs=(tile, tile, tile, flat, flat, flat, P()),
        out_specs=(tile, tile, tile),
        check_vma=False,
    )
```

```python
import functools

import jax
import jax.numpy as jnp
import numpy as np
from jax import lax
from jax.experimental import pallas as pl
from jax.experimental.pallas import tpu as pltpu
from jax.sharding import PartitionSpec as P

STEPS = 3
ITERS = 2
LWIDTH = 32
LSCALE = 12

LANES = 128
SUB = 8
SLOT = 16
EAST, SIDE = 2 * STEPS, 2 * STEPS - 1
PACK = LANES // SLOT
FOLD = LANES // LWIDTH
SHARES = (0.6, 0.4)

VMEM = pl.BlockSpec(memory_space=pltpu.VMEM)
SMEM = pl.BlockSpec(memory_space=pltpu.SMEM)
GRANT = pltpu.CompilerParams(vmem_limit_bytes=16 << 20)


def f32(*shape):
    return jax.ShapeDtypeStruct(shape, jnp.float32)


def iota(shape, axis):
    return lax.broadcasted_iota(jnp.int32, shape, axis)


def spin(block, shift, axis):
    shift %= block.shape[axis]
    return block if shift == 0 else pltpu.roll(block, shift, axis)


def shifted(block, axis, step, periodic):
    count = lax.axis_size(axis)
    if periodic:
        pairs = [(i, (i + step) % count) for i in range(count)]
    else:
        pairs = [(i, i + step) for i in range(count) if 0 <= i + step < count]
    return lax.ppermute(block, axis, pairs)


def everywhere_sum(block):
    half = jnp.zeros_like(block)
    for axis in ("band", "member"):
        count = lax.axis_size(axis)
        if count & (count - 1):
            block, half = lax.psum(block + half, axis), jnp.zeros_like(block)
            continue
        reach = 1
        while reach < count:
            block = block + half
            half = lax.ppermute(block, axis, [(i, i ^ reach) for i in range(count)])
            reach *= 2
    return jnp.stack([block, half])


def taper(offset):
    scaled = offset.astype(np.float32) / np.float32(LSCALE)
    weight = np.exp(np.float32(-0.5) * scaled * scaled)
    return np.where(np.abs(offset) <= LWIDTH, weight, np.float32(0)).astype(np.float32)


def two_terms(table):
    high = table.astype(jnp.bfloat16)
    low = (table - high.astype(np.float32)).astype(jnp.bfloat16)
    return high, low


def row_table(rows):
    out = np.arange(rows)[:, None]
    table = taper(np.arange(rows + 2 * LWIDTH)[None, :] - LWIDTH - out)
    high, low = two_terms(table)
    return np.block([[high, high], [low, np.zeros_like(low)]])


def column_table(cols):
    out = np.arange(cols)
    high, low = two_terms(taper(out[:, None] - out[None, :]))
    return np.block([[high, low], [high, np.zeros_like(low)]])


def strip_table(cols):
    near = np.arange(LWIDTH)
    left = taper((near - LWIDTH)[:, None] - near[None, :])
    right = taper((cols + near)[:, None] - (cols - LWIDTH + near)[None, :])
    table = np.zeros((2 * LANES, 2 * LANES), np.float32)
    for k in range(FOLD):
        src, dst = k * LWIDTH, 2 * k * LWIDTH
        table[src : src + LWIDTH, dst + LWIDTH : dst + 2 * LWIDTH] = left
        table[LANES + src : LANES + src + LWIDTH, dst : dst + LWIDTH] = right
    return two_terms(table)


def split(block):
    high = block.astype(jnp.bfloat16)
    low = (block - high.astype(jnp.float32)).astype(jnp.bfloat16)
    return high, low


def mm(a, b):
    return jnp.dot(a, b, preferred_element_type=jnp.float32)


SEAM = SLOT // 2


def slot_pack(block, k):
    lane = iota(block.shape, 1) // SLOT
    return jnp.where(lane == k, spin(block, SLOT * k + SEAM, 1), 0.0)


def row_pack_kernel(u_ref, v_ref, h_ref, top_ref, bottom_ref):
    members, rows, _ = u_ref.shape
    sub = iota((SUB, LANES), 0)
    last = slice(rows - SUB, rows)

    def member(k, _):
        u = u_ref[k, :SUB]
        top_ref[k, :SUB] = jnp.where(sub < 6, v_ref[k, :SUB], spin(u, 6, 0))
        top_ref[k, SUB:] = jnp.where(sub < 5, h_ref[k, :SUB], spin(u, 3, 0))
        u = u_ref[k, last]
        bottom_ref[k, :SUB] = jnp.where(sub < 2, spin(u, 5, 0), v_ref[k, last])
        bottom_ref[k, SUB:] = jnp.where(sub < 3, spin(u, 3, 0), h_ref[k, last])
        return 0

    lax.fori_loop(0, members, member, 0, unroll=8)


def pack_rows(height, eastward, northward):
    members, rows, cols = height.shape
    return pl.pallas_call(
        row_pack_kernel,
        name="pack_rows",
        compiler_params=GRANT,
        in_specs=[VMEM] * 3,
        out_specs=[VMEM] * 2,
        out_shape=[f32(members, 2 * SUB, cols)] * 2,
    )(eastward, northward, height)


def column_pack_kernel(u_ref, v_ref, h_ref, left_ref, right_ref, *own_refs):
    members, rows, _ = u_ref.shape
    slot = iota((rows, LANES), 1) % SLOT

    def group(g, _):
        packs = []
        for ref, own in zip((u_ref, v_ref, h_ref), own_refs):
            pack = slot_pack(ref[g * PACK], 0)
            for k in range(1, PACK):
                pack = pack + slot_pack(ref[g * PACK + k], k)
            own[g] = pack
            packs.append(pack)

        def sent(starts):
            u, v, h = (spin(p, at - start, 1) for p, start, at in zip(packs, starts, PLACES))
            return jnp.where(slot < PLACES[1], u, jnp.where(slot < PLACES[2], v, h))

        left_ref[g] = sent((SEAM, SEAM, SEAM))
        right_ref[g] = sent((SEAM - EAST, SEAM - SIDE, SEAM - SIDE))
        return 0

    lax.fori_loop(0, members // PACK, group, 0)


PLACES = (0, EAST, EAST + SIDE)


def pack_columns(height, eastward, northward):
    members, rows, cols = height.shape
    groups = members // PACK
    return pl.pallas_call(
        column_pack_kernel,
        name="pack_columns",
        compiler_params=GRANT,
        in_specs=[VMEM] * 3,
        out_specs=[VMEM] * 5,
        out_shape=[f32(groups, rows, LANES)] * 5,
    )(eastward, northward, height)


def difference_table(cols):
    lane = np.arange(cols)
    inner = (lane[:, None] == lane[None, :] + 1).astype(np.float32)
    inner -= lane[:, None] == lane[None, :] - 1
    wall = np.zeros((LANES, cols), np.float32)
    wall[SEAM - 1 :: SLOT, 0] = -1
    wall[SEAM::SLOT, cols - 1] = 1
    return np.concatenate([inner, inner, wall, wall]).astype(jnp.bfloat16)


def slot_masks(tall):
    lane = np.arange(LANES) // SLOT
    masks = lane[None, None, :] == np.arange(PACK)[:, None, None]
    return np.broadcast_to(masks, (PACK, tall, LANES)).astype(jnp.bfloat16)


def forecast_kernel(
    h_ref, u_ref, v_ref, above_ref, below_ref, ownu_ref, ownv_ref, ownh_ref, hall_ref, halr_ref,
    cornu_ref, cornd_ref, table_ref, mask_ref, edge_ref,
    ho_ref, uo_ref, vo_ref, mean_ref,
    us_ref, vs_ref, hs_ref, lhs_ref, sum_ref,
):
    members, rows, cols = h_ref.shape
    groups = members // PACK
    tall = rows + 2 * SUB
    batch = PACK + 2
    half = batch // 2
    slot = iota((tall, LANES), 1) % SLOT
    row = iota((tall, LANES), 0)
    sub = iota((SUB, LANES), 0)
    outside = ((row < SUB) & (edge_ref[0] == 1)) | ((row >= rows + SUB) & (edge_ref[1] == 1))
    pull = jnp.where(outside, 0.0, 0.2)
    mid, low, high = slice(SUB, SUB + tall), slice(SUB - 1, SUB + tall - 1), slice(SUB + 1, SUB + tall + 1)
    core = slice(2 * SUB, 2 * SUB + rows)

    def differences(ref):
        wall = jnp.where(slot == SEAM - 1, ref[PACK, mid], ref[PACK + 1, mid])
        walls = split(wall)
        for j in range(batch):
            for i, part in enumerate(split(ref[j, mid])):
                lhs_ref[j, :, i * LANES : (i + 1) * LANES] = part
            if j < PACK:
                for i, part in enumerate(walls):
                    lhs_ref[j, :, (i + 2) * LANES : (i + 3) * LANES] = part * mask_ref[j]
        out = []
        for start in (0, half):
            stack = lhs_ref[start : start + half].reshape(half * tall, 4 * LANES)
            d = mm(stack, table_ref[...])
            out += [d[j * tall : (j + 1) * tall] for j in range(half)]
        return out

    def group(g, _):
        packs = [[None] * 2 for _ in range(3)]
        for k in range(PACK):
            m = g * PACK + k
            a0, a1 = above_ref[m, :SUB], above_ref[m, SUB:]
            b0, b1 = below_ref[m, :SUB], below_ref[m, SUB:]
            ua = jnp.where(sub < 5, spin(a0, 3, 0), spin(a1, 5, 0))
            ub = jnp.where(sub < 2, spin(b0, 2, 0), spin(b1, 5, 0))
            ends = ((us_ref, ua, ub, u_ref), (vs_ref, a0, b0, v_ref), (hs_ref, a1, b1, h_ref))
            for i, (state, a, b, ref) in enumerate(ends):
                state[k, SUB : 2 * SUB] = a
                state[k, core] = ref[m]
                state[k, 2 * SUB + rows : 3 * SUB + rows] = b
                for end, edge in enumerate((a, b)):
                    piece = slot_pack(edge, k)
                    packs[i][end] = piece if k == 0 else packs[i][end] + piece
        left = jnp.concatenate([cornu_ref[g], hall_ref[g], cornd_ref[g]], axis=0)
        right = jnp.concatenate([cornu_ref[groups + g], halr_ref[g], cornd_ref[groups + g]], axis=0)
        owns = ((us_ref, ownu_ref, EAST), (vs_ref, ownv_ref, SIDE), (hs_ref, ownh_ref, SIDE))
        for i, (state, own_ref, size) in enumerate(owns):
            own = jnp.concatenate([packs[i][0], own_ref[g], packs[i][1]], axis=0)
            state[PACK, mid] = jnp.where(slot < SEAM, spin(left, SEAM - size - PLACES[i], 1), own)
            state[PACK + 1, mid] = jnp.where(slot < SEAM, own, spin(right, SEAM - PLACES[i], 1))

        for step in range(STEPS):
            last = step == STEPS - 1
            for j, d in enumerate(differences(us_ref)):
                hs_ref[j, mid] = hs_ref[j, mid] - pull * (d + (vs_ref[j, high] - vs_ref[j, low]))
            for j, d in enumerate(differences(hs_ref)):
                if last and j >= PACK:
                    continue
                u, v = us_ref[j, mid], vs_ref[j, mid]
                us_ref[j, mid] = u + 0.1 * v - pull * d
                vs_ref[j, mid] = v - 0.1 * u - pull * (hs_ref[j, high] - hs_ref[j, low])

        for i, (state, out) in enumerate(((hs_ref, ho_ref), (us_ref, uo_ref), (vs_ref, vo_ref))):
            total = sum_ref[i]
            for k in range(PACK):
                x = state[k, core]
                out[g * PACK + k] = x
                total = total + x
            sum_ref[i] = total
        return 0

    sum_ref[...] = jnp.zeros_like(sum_ref)
    lhs_ref[...] = jnp.zeros_like(lhs_ref)
    for state in (us_ref, vs_ref, hs_ref):
        for j in range(batch):
            state[j, :SUB] = jnp.zeros((SUB, LANES), jnp.float32)
            state[j, SUB + tall :] = jnp.zeros((SUB, LANES), jnp.float32)
    lax.fori_loop(0, groups, group, 0)
    for i in range(3):
        mean_ref[i] = sum_ref[i] / members


def forecast(h, u, v, *rest):
    members, rows, cols = h.shape
    tall = rows + 2 * SUB
    state = pltpu.VMEM((PACK + 2, tall + 2 * SUB, LANES), jnp.float32)
    *halos, edge = rest
    return pl.pallas_call(
        forecast_kernel,
        name="forecast",
        compiler_params=GRANT,
        in_specs=[VMEM] * (len(halos) + 5) + [SMEM],
        out_specs=[VMEM] * 4,
        out_shape=[f32(members, rows, cols)] * 3 + [f32(3, rows, cols)],
        scratch_shapes=[
            state,
            state,
            state,
            pltpu.VMEM((PACK + 2, tall, 4 * LANES), jnp.bfloat16),
            pltpu.VMEM((3, rows, cols), jnp.float32),
        ],
    )(h, u, v, *halos, difference_table(cols), slot_masks(tall), edge)


def factor(square_ref, step_ref, cells):
    total = jnp.sum(square_ref[0] + square_ref[1], keepdims=True)
    return step_ref[0] / jnp.sqrt(total / cells + 1e-06)


def contrib_kernel(begin, cells, h_ref, u_ref, v_ref, mean_ref, obs_ref, *refs):
    if len(refs) == 1:
        (contrib_ref,) = refs
        states = means = [mean_ref[i] for i in range(3)]
    else:
        sums_ref, square_ref, step_ref, contrib_ref = refs
        means = [mean_ref[i] for i in range(3)]
        f = factor(square_ref, step_ref, cells)
        states = [means[i] + f * sums_ref[i] for i in range(3)]
    members = h_ref.shape[0]
    scale = 1.0 / float(np.sqrt(np.float32(members - 1)))
    sh, su, sv = states
    residual = obs_ref[1] * (obs_ref[0] - sh - 0.15 * (su * su + sv * sv))
    residual = residual * scale
    eu, ev = 0.3 * su, 0.3 * sv
    mh, mu, mv = means

    def member(m, _):
        h, u, v = (ref[begin + m] for ref in (h_ref, u_ref, v_ref))
        contrib_ref[m] = ((h - mh) + (eu * (u - mu) + ev * (v - mv))) * residual
        return 0

    lax.fori_loop(0, contrib_ref.shape[0], member, 0, unroll=4)


def contributions(part, cells, fields, means, obs, *more):
    begin, count = part
    return pl.pallas_call(
        functools.partial(contrib_kernel, begin, cells),
        name="contributions",
        compiler_params=GRANT,
        in_specs=[VMEM] * 5 + ([VMEM, VMEM, SMEM] if more else []),
        out_specs=VMEM,
        out_shape=f32(count, *fields[0].shape[1:]),
    )(*fields, means, obs, *more)


def rows_kernel(x_ref, above_ref, below_ref, table_ref, out_ref, left_ref, right_ref):
    members, rows, cols = x_ref.shape
    lane = iota((rows, LANES), 1)
    table = table_ref[...]

    def fold(g, _):
        left = right = None
        for pair in range(FOLD // 2):
            halves = []
            for k in (2 * pair, 2 * pair + 1):
                m = g * FOLD + k
                high, low = split(jnp.concatenate([above_ref[m], x_ref[m], below_ref[m]], axis=0))
                halves.append(jnp.concatenate([high, low], axis=0))
            both = mm(table, jnp.concatenate(halves, axis=1))
            both = both[:rows] + both[rows:]
            for k in (2 * pair, 2 * pair + 1):
                y = both[:, (k % 2) * cols : (k % 2 + 1) * cols]
                out_ref[g * FOLD + k] = y
                here = lane // LWIDTH == k
                l = jnp.where(here, spin(y, LWIDTH * k, 1), 0.0)
                r = jnp.where(here, spin(y, LWIDTH * k + LWIDTH - cols, 1), 0.0)
                left, right = (l, r) if k == 0 else (left + l, right + r)
        left_ref[g] = left
        right_ref[g] = right
        return 0

    lax.fori_loop(0, members // FOLD, fold, 0, unroll=2)


def taper_rows(x, above, below):
    members, rows, cols = x.shape
    folds = members // FOLD
    return pl.pallas_call(
        rows_kernel,
        name="taper_rows",
        compiler_params=GRANT,
        in_specs=[VMEM] * 4,
        out_specs=[VMEM] * 3,
        out_shape=[f32(members, rows, cols)] + [f32(folds, rows, LANES)] * 2,
    )(x, above, below, row_table(rows))


def columns_kernel(begin, cells, kinds, *refs):
    names = dict(zip(kinds, refs))
    x_ref, left_ref, right_ref = (names[n] for n in ("x", "left", "right"))
    mean_ref, sums_ref, square_ref = (names[n] for n in ("means", "sums", "square"))
    grad_ref = names["grad"]
    fields = [names[n] for n in "huv"]
    count, rows, cols = x_ref.shape
    scale = 1.0 / float(np.sqrt(np.float32(fields[0].shape[0] - 1)))
    lane = iota((rows, LANES), 1)
    rim = (lane < LWIDTH) | (lane >= cols - LWIDTH)

    def fold(g, _):
        xh, xl = split(jnp.concatenate([left_ref[g], right_ref[g]], axis=1))
        high_table = names["high"][...]
        strips = mm(xh, high_table) + (mm(xl, high_table) + mm(xh, names["low"][...]))
        block = jnp.concatenate([x_ref[g * FOLD + k] for k in range(FOLD)], axis=0)
        bh, bl = split(block)
        both = mm(jnp.concatenate([bh, bl], axis=1), names["table"][...])
        both = both[:, :cols] + both[:, cols:]
        for k in range(FOLD):
            at = 2 * k * LWIDTH
            part = strips[:, at // LANES * LANES : at // LANES * LANES + LANES]
            part = spin(part, -(at % LANES + LWIDTH), 1)
            y = both[k * rows : (k + 1) * rows] + jnp.where(rim, part, 0.0)
            grad_ref[g * FOLD + k] = y
        return 0

    lax.fori_loop(0, count // FOLD, fold, 0, unroll=2)
    zero = jnp.zeros((SUB, cols), jnp.float32)
    square = names["square0"][...] if "square0" in names else zero
    if "prev" in names:
        f = factor(names["squares"], names["step"], cells)
    for start in range(0, rows, SUB):
        part = slice(start, start + SUB)
        means = [mean_ref[i, part] for i in range(3)]

        def member(m, carry):
            square, *sums = carry
            y = grad_ref[m, part]
            if "prev" in names:
                y = f * names["prev"][m, part] - y
            square = square + y * y
            terms = ((ref[begin + m, part] - mean) * y for ref, mean in zip(fields, means))
            return (square, *(s + t for s, t in zip(sums, terms)))

        square, *sums = lax.fori_loop(0, count, member, (square, zero, zero, zero), unroll=4)
        for i in range(3):
            total = sums[i] * scale
            if "sums0" in names:
                total = total + names["sums0"][i, part]
            sums_ref[i, part] = total
    square_ref[...] = square


def taper_columns(part, cells, x, left, right, fields, means, carried, before):
    count, rows, cols = x.shape
    high, low = strip_table(cols)
    ins = dict(x=x, left=left, right=right, means=means, table=column_table(cols), high=high, low=low)
    ins.update(zip("huv", fields))
    if carried:
        ins.update(sums0=carried[0], square0=carried[1])
    if before:
        ins.update(prev=before[0], squares=before[1], step=before[2])
    grad = f32(count, rows, cols)
    outs = dict(sums=f32(3, rows, cols), square=f32(SUB, LANES))
    if not before:
        outs["grad"] = grad
    kinds = (*ins, *outs, *(() if "grad" in outs else ("grad",)))
    result = pl.pallas_call(
        functools.partial(columns_kernel, part[0], cells, kinds),
        name="taper_columns",
        compiler_params=GRANT,
        in_specs=[SMEM if n == "step" else VMEM for n in ins],
        out_specs=[VMEM] * len(outs),
        out_shape=list(outs.values()),
        scratch_shapes=[] if "grad" in outs else [pltpu.VMEM(grad.shape, jnp.float32)],
    )(*ins.values())
    return result[:2], result[2:]


def analysis_kernel(cells, h_ref, u_ref, v_ref, *refs):
    s0_ref, s1_ref, q0_ref, q1_ref, step0_ref, step1_ref, *outs, increment_ref = refs

    @pl.when(pl.program_id(0) == 0)
    def _():
        f0, f1 = factor(q0_ref, step0_ref, cells), factor(q1_ref, step1_ref, cells)
        increment_ref[...] = f0 * s0_ref[...] - f1 * s1_ref[...]

    begin = pl.program_id(0) * outs[0].shape[0]
    for i, (ref, out) in enumerate(zip((h_ref, u_ref, v_ref), outs)):
        for k in range(outs[0].shape[0]):
            out[k] = ref[begin + k] + increment_ref[i]


def analysis(cells, fields, *rest):
    members, rows, cols = fields[0].shape
    block = pl.BlockSpec((2 * PACK, rows, cols), lambda g: (g, 0, 0))
    return pl.pallas_call(
        functools.partial(analysis_kernel, cells),
        name="analysis",
        compiler_params=GRANT,
        grid=(members // (2 * PACK),),
        in_specs=[VMEM] * 7 + [SMEM] * 2,
        out_specs=[block] * 3,
        out_shape=[f32(members, rows, cols)] * 3,
        scratch_shapes=[pltpu.VMEM((3, rows, cols), jnp.float32)],
    )(*fields, *rest)


def parts_of(members):
    sizes, left = [], members // FOLD
    for share in SHARES[:-1]:
        sizes.append(int(round(share * members / FOLD)))
        left -= sizes[-1]
    sizes.append(left)
    begins = np.cumsum([0] + sizes[:-1])
    return [(int(b) * FOLD, n * FOLD) for b, n in zip(begins, sizes) if n]


def per_device(
    height_start, east_start, north_start, obs_value, obs_mask, obs_precision, step_sizes
):
    members, rows, cols = height_start.shape
    starts = (height_start, east_start, north_start)
    top, bottom = pack_rows(*starts)
    above = shifted(bottom, "member", 1, False)
    below = shifted(top, "member", -1, False)
    starts, bottom = lax.optimization_barrier((starts, bottom))
    first, last, *own = pack_columns(*starts)
    hall = shifted(last, "band", 1, True)
    halr = shifted(first, "band", -1, True)
    ends = jnp.concatenate([hall, halr], axis=0)
    cornu = shifted(ends[:, rows - SUB :], "member", 1, False)
    cornd = shifted(ends[:, :SUB], "member", -1, False)

    obs = jnp.stack([obs_value, obs_mask.astype(jnp.float32) * obs_precision])
    here = lax.axis_index("member")
    edge = jnp.stack([here == 0, here == lax.axis_size("member") - 1]).astype(jnp.int32)
    *fields, means = forecast(*starts, above, below, *own, hall, halr, cornu, cornd, edge)
    cells = float(members * rows * cols * lax.axis_size("member") * lax.axis_size("band"))
    parts = parts_of(members)
    steps = [(step_sizes[k : k + 1].astype(jnp.float32) / 64.0) for k in range(ITERS)]

    def localized(contribs, before):
        sent = [
            (shifted(c, "member", 1, False), shifted(c, "member", -1, False)) for c in contribs
        ]
        tapered = []
        for c, (above, below) in zip(contribs, sent):
            x, first, last = taper_rows(c, above, below)
            tapered.append((x, shifted(last, "band", 1, True), shifted(first, "band", -1, True)))
        carried, grads = (), []
        for i, (part, arrays) in enumerate(zip(parts, tapered)):
            more = (before[0][i], *before[1:]) if before else ()
            carried, grad = taper_columns(part, cells, *arrays, fields, means, carried, more)
            grads += grad
        return carried[0], everywhere_sum(carried[1]), grads

    first = [contributions(part, cells, fields, means, obs) for part in parts]
    sums0, squares0, grads = localized(first, ())
    second = [
        contributions(part, cells, fields, means, obs, sums0, squares0, steps[0]) for part in parts
    ]
    sums1, squares1, _ = localized(second, (grads, squares0, steps[0]))
    return tuple(analysis(cells, fields, sums0, sums1, squares0, squares1, *steps))


def solution(mesh):
    tile, flat = P(None, "member", "band"), P("member", "band")
    return jax.shard_map(
        per_device,
        mesh=mesh,
        in_specs=(tile, tile, tile, flat, flat, flat, P()),
        out_specs=(tile, tile, tile),
        check_vma=False,
    )
```

```python
import functools

import jax
import jax.numpy as jnp
import numpy as np
from jax import lax
from jax.experimental import pallas as pl
from jax.experimental.pallas import tpu as pltpu
from jax.sharding import PartitionSpec as P


STEPS = 3
LWIDTH = 32
LSCALE = 12

LANES = 128
SUB = 8
SLOT = 16
EAST, SIDE = 2 * STEPS, 2 * STEPS - 1
PACK = LANES // SLOT
FOLD = LANES // LWIDTH
SHARES = (0.6, 0.4)

VMEM = pl.BlockSpec(memory_space=pltpu.VMEM)
SMEM = pl.BlockSpec(memory_space=pltpu.SMEM)
GRANT = pltpu.CompilerParams(vmem_limit_bytes=16 << 20)


def f32(*shape):
    return jax.ShapeDtypeStruct(shape, jnp.float32)


def iota(shape, axis):
    return lax.broadcasted_iota(jnp.int32, shape, axis)


def spin(block, shift, axis):
    shift %= block.shape[axis]
    return block if shift == 0 else pltpu.roll(block, shift, axis)


def shifted(block, axis, step, periodic):
    count = lax.axis_size(axis)
    if periodic:
        pairs = [(i, (i + step) % count) for i in range(count)]
    else:
        pairs = [(i, i + step) for i in range(count) if 0 <= i + step < count]
    return lax.ppermute(block, axis, pairs)


def everywhere_sum(block):
    half = jnp.zeros_like(block)
    for axis in ("band", "member"):
        count = lax.axis_size(axis)
        if count & (count - 1):
            block, half = lax.psum(block + half, axis), jnp.zeros_like(block)
            continue
        reach = 1
        while reach < count:
            block = block + half
            half = lax.ppermute(block, axis, [(i, i ^ reach) for i in range(count)])
            reach *= 2
    return block, half


def taper(offset):
    scaled = offset.astype(np.float32) / np.float32(LSCALE)
    weight = np.exp(np.float32(-0.5) * scaled * scaled)
    return np.where(np.abs(offset) <= LWIDTH, weight, np.float32(0)).astype(np.float32)


def two_terms(table):
    high = table.astype(jnp.bfloat16)
    low = (table - high.astype(np.float32)).astype(jnp.bfloat16)
    return high, low


def row_table(rows):
    out = np.arange(rows)[:, None]
    table = taper(np.arange(rows + 2 * LWIDTH)[None, :] - LWIDTH - out)
    high, low = two_terms(table)
    return np.block([[high, high], [low, np.zeros_like(low)]])


def column_table(cols):
    out = np.arange(cols)
    high, low = two_terms(taper(out[:, None] - out[None, :]))
    return np.block([[high, low], [high, np.zeros_like(low)]])


def strip_table(cols):
    near = np.arange(LWIDTH)
    left = taper((near - LWIDTH)[:, None] - near[None, :])
    right = taper((cols + near)[:, None] - (cols - LWIDTH + near)[None, :])
    table = np.zeros((2 * LANES, 2 * LANES), np.float32)
    for k in range(FOLD):
        src, dst = k * LWIDTH, 2 * k * LWIDTH
        table[src : src + LWIDTH, dst + LWIDTH : dst + 2 * LWIDTH] = left
        table[LANES + src : LANES + src + LWIDTH, dst : dst + LWIDTH] = right
    return two_terms(table)


def split(block):
    high = block.astype(jnp.bfloat16)
    low = (block - high.astype(jnp.float32)).astype(jnp.bfloat16)
    return high, low


def mm(a, b):
    return jnp.dot(a, b, preferred_element_type=jnp.float32)


SEAM = SLOT // 2


def slot_pack(block, k):
    lane = iota(block.shape, 1) // SLOT
    return jnp.where(lane == k, spin(block, SLOT * k + SEAM, 1), 0.0)


def row_pack_kernel(uf_ref, vf_ref, hf_ref, ul_ref, vl_ref, hl_ref, top_ref, bottom_ref):
    sub = iota((SUB, LANES), 0)

    def member(k, _):
        u = uf_ref[k]
        top_ref[k, :SUB] = jnp.where(sub < 6, vf_ref[k], spin(u, 6, 0))
        top_ref[k, SUB:] = jnp.where(sub < 5, hf_ref[k], spin(u, 3, 0))
        u = ul_ref[k]
        bottom_ref[k, :SUB] = jnp.where(sub < 2, spin(u, 5, 0), vl_ref[k])
        bottom_ref[k, SUB:] = jnp.where(sub < 3, spin(u, 3, 0), hl_ref[k])
        return 0

    lax.fori_loop(0, uf_ref.shape[0], member, 0, unroll=4)


def pack_rows(height, eastward, northward):
    members, rows, cols = height.shape
    count = members // 2
    first = pl.BlockSpec((count, SUB, cols), lambda g: (g, 0, 0))
    last = pl.BlockSpec((count, SUB, cols), lambda g: (g, rows // SUB - 1, 0))
    edge = pl.BlockSpec((count, 2 * SUB, cols), lambda g: (g, 0, 0))
    fields = (eastward, northward, height)
    return pl.pallas_call(
        row_pack_kernel,
        name="pack_rows",
        grid=(members // count,),
        in_specs=[first] * 3 + [last] * 3,
        out_specs=[edge] * 2,
        out_shape=[f32(members, 2 * SUB, cols)] * 2,
    )(*fields, *fields)


def column_pack_kernel(u_ref, v_ref, h_ref, left_ref, right_ref, *refs):
    own_refs, kept_refs = refs[:3], refs[3:]
    members, rows, _ = u_ref.shape
    slot = iota((rows, LANES), 1) % SLOT

    def group(g, _):
        packs = []
        for ref, own, kept in zip((u_ref, v_ref, h_ref), own_refs, kept_refs):
            pack = None
            for k in range(PACK):
                x = ref[g * PACK + k]
                kept[g * PACK + k] = x
                piece = slot_pack(x, k)
                pack = piece if k == 0 else pack + piece
            own[g] = pack
            packs.append(pack)

        def sent(starts):
            u, v, h = (spin(p, at - start, 1) for p, start, at in zip(packs, starts, PLACES))
            return jnp.where(slot < PLACES[1], u, jnp.where(slot < PLACES[2], v, h))

        left_ref[g] = sent((SEAM, SEAM, SEAM))
        right_ref[g] = sent((SEAM - EAST, SEAM - SIDE, SEAM - SIDE))
        return 0

    lax.fori_loop(0, members // PACK, group, 0)


PLACES = (0, EAST, EAST + SIDE)


def pack_columns(height, eastward, northward):
    members, rows, cols = height.shape
    groups = members // PACK
    return pl.pallas_call(
        column_pack_kernel,
        name="pack_columns",
        compiler_params=GRANT,
        in_specs=[VMEM] * 3,
        out_specs=[VMEM] * 8,
        out_shape=[f32(groups, rows, LANES)] * 5 + [f32(members, rows, cols)] * 3,
    )(eastward, northward, height)


def difference_table(cols):
    lane = np.arange(cols)
    table = (lane[:, None] == lane[None, :] + 1).astype(np.float32)
    table -= lane[:, None] == lane[None, :] - 1
    return np.concatenate([table, table]).astype(jnp.bfloat16)


def forecast_kernel(
    h_ref, u_ref, v_ref, above_ref, below_ref, ownu_ref, ownv_ref, ownh_ref, hall_ref, halr_ref,
    cornu_ref, cornd_ref, table_ref,
    ho_ref, uo_ref, vo_ref, mean_ref,
    us_ref, vs_ref, hs_ref, lhs_ref, sum_ref,
):
    _, rows, _ = h_ref.shape
    groups = pl.num_programs(0)
    members = groups * PACK
    tall = rows + 2 * SUB
    batch = PACK + 2
    half = batch // 2
    slot = iota((tall, LANES), 1) % SLOT
    row = iota((tall, LANES), 0)
    sub = iota((SUB, LANES), 0)
    here, tiles = lax.axis_index("member"), lax.axis_size("member")
    outside = ((row < SUB) & (here == 0)) | ((row >= rows + SUB) & (here == tiles - 1))
    pull = jnp.where(outside, 0.0, 0.2)
    mid, low, high = slice(SUB, SUB + tall), slice(SUB - 1, SUB + tall - 1), slice(SUB + 1, SUB + tall + 1)
    core = slice(2 * SUB, 2 * SUB + rows)

    ends = (iota((tall, LANES), 1) == 0) | (iota((tall, LANES), 1) == LANES - 1)
    order = (PACK, PACK + 1, *range(PACK))

    def differences(ref):
        right = spin(ref[PACK + 1, mid], -2, 1)
        wall = jnp.where(slot == SEAM - 1, -ref[PACK, mid], right)
        for start in (0, half):
            for at, j in enumerate(order[start : start + half], start):
                for i, part in enumerate(split(ref[j, mid])):
                    lhs_ref[at, :, i * LANES : (i + 1) * LANES] = part
            stack = lhs_ref[start : start + half].reshape(half * tall, 2 * LANES)
            d = mm(stack, table_ref[...])
            for at, j in enumerate(order[start : start + half]):
                piece = d[at * tall : (at + 1) * tall]
                if j < PACK:
                    piece += jnp.where(ends, spin(wall, -(SLOT * j + SEAM - 1), 1), 0.0)
                yield j, piece

    def group():
        packs = [[None] * 2 for _ in range(3)]
        for k in range(PACK):
            m = k
            a0, a1 = above_ref[m, :SUB], above_ref[m, SUB:]
            b0, b1 = below_ref[m, :SUB], below_ref[m, SUB:]
            ua = jnp.where(sub < 5, spin(a0, 3, 0), spin(a1, 5, 0))
            ub = jnp.where(sub < 2, spin(b0, 2, 0), spin(b1, 5, 0))
            ends = ((us_ref, ua, ub, u_ref), (vs_ref, a0, b0, v_ref), (hs_ref, a1, b1, h_ref))
            for i, (state, a, b, ref) in enumerate(ends):
                state[k, SUB : 2 * SUB] = a
                state[k, core] = ref[m]
                state[k, 2 * SUB + rows : 3 * SUB + rows] = b
                for end, edge in enumerate((a, b)):
                    piece = slot_pack(edge, k)
                    packs[i][end] = piece if k == 0 else packs[i][end] + piece
        left = jnp.concatenate([cornu_ref[0, 0], hall_ref[0], cornd_ref[0, 0]], axis=0)
        right = jnp.concatenate([cornu_ref[1, 0], halr_ref[0], cornd_ref[1, 0]], axis=0)
        owns = ((us_ref, ownu_ref, EAST), (vs_ref, ownv_ref, SIDE), (hs_ref, ownh_ref, SIDE))
        for i, (state, own_ref, size) in enumerate(owns):
            own = jnp.concatenate([packs[i][0], own_ref[0], packs[i][1]], axis=0)
            state[PACK, mid] = jnp.where(slot < SEAM, spin(left, SEAM - size - PLACES[i], 1), own)
            state[PACK + 1, mid] = jnp.where(slot < SEAM, own, spin(right, SEAM - PLACES[i], 1))

        for step in range(STEPS):
            last = step == STEPS - 1
            for j, d in differences(us_ref):
                hs_ref[j, mid] = hs_ref[j, mid] - pull * (d + (vs_ref[j, high] - vs_ref[j, low]))
            for j, d in differences(hs_ref):
                if last and j >= PACK:
                    continue
                u, v = us_ref[j, mid], vs_ref[j, mid]
                us_ref[j, mid] = u + 0.1 * v - pull * d
                vs_ref[j, mid] = v - 0.1 * u - pull * (hs_ref[j, high] - hs_ref[j, low])

        for i, (state, out) in enumerate(((hs_ref, ho_ref), (us_ref, uo_ref), (vs_ref, vo_ref))):
            total = sum_ref[i]
            for k in range(PACK):
                x = state[k, core]
                out[k] = x
                total = total + x
            sum_ref[i] = total

    @pl.when(pl.program_id(0) == 0)
    def _():
        sum_ref[...] = jnp.zeros_like(sum_ref)
        for state in (us_ref, vs_ref, hs_ref):
            for j in range(batch):
                state[j, :SUB] = jnp.zeros((SUB, LANES), jnp.float32)
                state[j, SUB + tall :] = jnp.zeros((SUB, LANES), jnp.float32)

    group()

    @pl.when(pl.program_id(0) == groups - 1)
    def _():
        for i in range(3):
            mean_ref[i] = sum_ref[i] * (1.0 / members)


def forecast(h, u, v, above, below, *rest):
    members, rows, cols = h.shape
    groups = members // PACK
    tall = rows + 2 * SUB
    state = pltpu.VMEM((PACK + 2, tall + 2 * SUB, LANES), jnp.float32)
    *strips, cornu, cornd = rest
    cornu, cornd = (x.reshape(2, groups, SUB, LANES) for x in (cornu, cornd))
    tile = pl.BlockSpec((PACK, rows, cols), lambda g: (g, 0, 0))
    side = pl.BlockSpec((PACK, 2 * SUB, cols), lambda g: (g, 0, 0))
    strip = pl.BlockSpec((1, rows, LANES), lambda g: (g, 0, 0))
    corner = pl.BlockSpec((2, 1, SUB, LANES), lambda g: (0, g, 0, 0))
    mean = pl.BlockSpec((3, rows, cols), lambda g: (0, 0, 0))
    return pl.pallas_call(
        forecast_kernel,
        name="forecast",
        compiler_params=GRANT,
        grid=(groups,),
        in_specs=[tile] * 3 + [side] * 2 + [strip] * 5 + [corner] * 2 + [VMEM],
        out_specs=[tile] * 3 + [mean],
        out_shape=[f32(members, rows, cols)] * 3 + [f32(3, rows, cols)],
        scratch_shapes=[
            state,
            state,
            state,
            pltpu.VMEM((PACK + 2, tall, 2 * LANES), jnp.bfloat16),
            pltpu.VMEM((3, rows, cols), jnp.float32),
        ],
    )(h, u, v, above, below, *strips, cornu, cornd, difference_table(cols))


def factor(k, square_ref, half_ref, step_ref, cells):
    total = jnp.sum(square_ref[...] + half_ref[...], keepdims=True)
    return step_ref[k].astype(jnp.float32) / 64.0 / jnp.sqrt(total / cells + 1e-06)


def slope_kernel(begin, h_ref, u_ref, v_ref, mean_ref, value_ref, seen_ref, precise_ref, *refs):
    *sums, out_ref = refs
    members = h_ref.shape[0]
    extra = 2 if sums else 1
    count = out_ref.shape[0] - (0 if begin else extra)
    scale = 1.0 / float(np.sqrt(np.float32(members - 1)))
    mh, mu, mv = (mean_ref[i] for i in range(3))
    value, weight = value_ref[...], seen_ref[...].astype(jnp.float32) * precise_ref[...]
    if sums:
        dh, du, dv = (sums[0][i] for i in range(3))
        eu, ev = (0.3 * scale) * du, (0.3 * scale) * dv
        rests = (
            -weight * (dh + 0.3 * (mu * du + mv * dv)),
            (-0.15 * weight) * (du * du + dv * dv),
        )
    else:
        eu, ev = (0.3 * scale) * mu, (0.3 * scale) * mv
        rests = (weight * (value - mh - 0.15 * (mu * mu + mv * mv)),)
    if not begin:
        for i, rest in enumerate(rests):
            out_ref[count + i] = rest

    def member(m, _):
        slope = eu * (u_ref[begin + m] - mu) + ev * (v_ref[begin + m] - mv)
        if not sums:
            slope = (h_ref[begin + m] - mh) * scale + slope
        out_ref[m] = slope
        return 0

    lax.fori_loop(0, count, member, 0, unroll=4)


def slopes(part, fields, means, obs, *sums):
    begin, count = part
    extra = 0 if begin else 1 + len(sums)
    return pl.pallas_call(
        functools.partial(slope_kernel, begin),
        name="slopes",
        compiler_params=GRANT,
        in_specs=[VMEM] * (7 + len(sums)),
        out_specs=VMEM,
        out_shape=f32(count + extra, *fields[0].shape[1:]),
    )(*fields, means, *obs, *sums)


def rows_kernel(cells, orders, shared, *refs):
    blocks = [refs[3 * i : 3 * i + 3] for i in range(orders)]
    refs = refs[3 * orders :]
    heads = [refs[3 * i : 3 * i + 3] for i in range(orders)] if shared else blocks
    refs = refs[3 * orders * shared :]
    *scales, table_ref, out_ref, left_ref, right_ref = refs
    members, rows, cols = out_ref.shape
    first = heads[0][0].shape[0] - 1
    lane = iota((rows, LANES), 1)
    table = table_ref[...]

    def tall(trio, m):
        own, above, below = trio
        return jnp.concatenate([above[m], own[m], below[m]], axis=0)

    rest = tall(heads[0], first)
    if orders > 1:
        f = factor(0, *scales, cells)
        rest = rest + f * (tall(heads[1], first) + f * tall(heads[1], first + 1))

    def fold(g, _):
        left = right = None
        for pair in range(FOLD // 2):
            halves = []
            for k in (2 * pair, 2 * pair + 1):
                m = g * FOLD + k
                slope = tall(blocks[0], m)
                if orders > 1:
                    slope = slope + f * tall(blocks[1], m)
                high, low = split(slope * rest)
                halves.append(jnp.concatenate([high, low], axis=0))
            both = mm(table, jnp.concatenate(halves, axis=1))
            both = both[:rows] + both[rows:]
            for k in (2 * pair, 2 * pair + 1):
                y = both[:, (k % 2) * cols : (k % 2 + 1) * cols]
                out_ref[g * FOLD + k] = y
                here = lane // LWIDTH == k
                l = jnp.where(here, spin(y, LWIDTH * k, 1), 0.0)
                r = jnp.where(here, spin(y, LWIDTH * k + LWIDTH - cols, 1), 0.0)
                left, right = (l, r) if k == 0 else (left + l, right + r)
        left_ref[g] = left
        right_ref[g] = right
        return 0

    lax.fori_loop(0, members // FOLD, fold, 0, unroll=2)


def taper_rows(part, cells, blocks, heads, scales):
    begin, members = part
    _, rows, cols = blocks[0][0].shape
    folds = members // FOLD
    shared = bool(begin)
    arrays = [x for trio in blocks + (heads if shared else []) for x in trio]
    return pl.pallas_call(
        functools.partial(rows_kernel, cells, len(blocks), shared),
        name="taper_rows",
        compiler_params=GRANT,
        in_specs=[VMEM] * len(arrays) + ([VMEM, VMEM, SMEM] if scales else []) + [VMEM],
        out_specs=[VMEM] * 3,
        out_shape=[f32(members, rows, cols)] + [f32(folds, rows, LANES)] * 2,
    )(*arrays, *scales, row_table(rows))


def columns_kernel(begin, cells, kinds, *refs):
    names = dict(zip(kinds, refs))
    x_ref, left_ref, right_ref = (names[n] for n in ("x", "left", "right"))
    mean_ref, sums_ref, square_ref = (names[n] for n in ("means", "sums", "square"))
    grad_ref = names["grad"]
    fields = [names[n] for n in "huv"]
    count, rows, cols = x_ref.shape
    scale = 1.0 / float(np.sqrt(np.float32(fields[0].shape[0] - 1)))
    lane = iota((rows, LANES), 1)
    rim = (lane < LWIDTH) | (lane >= cols - LWIDTH)

    def fold(g, _):
        xh, xl = split(jnp.concatenate([left_ref[g], right_ref[g]], axis=1))
        high_table = names["high"][...]
        strips = mm(xh, high_table) + (mm(xl, high_table) + mm(xh, names["low"][...]))
        block = jnp.concatenate([x_ref[g * FOLD + k] for k in range(FOLD)], axis=0)
        bh, bl = split(block)
        both = mm(jnp.concatenate([bh, bl], axis=1), names["table"][...])
        both = both[:, :cols] + both[:, cols:]
        for k in range(FOLD):
            at = 2 * k * LWIDTH
            part = strips[:, at // LANES * LANES : at // LANES * LANES + LANES]
            part = spin(part, -(at % LANES + LWIDTH), 1)
            y = both[k * rows : (k + 1) * rows] + jnp.where(rim, part, 0.0)
            grad_ref[g * FOLD + k] = y
        return 0

    lax.fori_loop(0, count // FOLD, fold, 0, unroll=2)
    zero = jnp.zeros((SUB, cols), jnp.float32)
    square = names["square0"][...] if "square0" in names else zero
    if "prev" in names:
        f = factor(0, names["total"], names["half"], names["step"], cells)
    for start in range(0, rows, SUB):
        part = slice(start, start + SUB)
        means = [mean_ref[i, part] for i in range(3)]

        def member(m, carry):
            square, *sums = carry
            y = grad_ref[m, part]
            if "prev" in names:
                y = f * names["prev"][m, part] - y
            square = square + y * y
            terms = ((ref[begin + m, part] - mean) * y for ref, mean in zip(fields, means))
            return (square, *(s + t for s, t in zip(sums, terms)))

        square, *sums = lax.fori_loop(0, count, member, (square, zero, zero, zero), unroll=4)
        for i in range(3):
            total = sums[i] * scale
            if "sums0" in names:
                total = total + names["sums0"][i, part]
            sums_ref[i, part] = total
    square_ref[...] = square


def taper_columns(part, cells, x, left, right, fields, means, carried, before):
    count, rows, cols = x.shape
    high, low = strip_table(cols)
    ins = dict(x=x, left=left, right=right, means=means, table=column_table(cols), high=high, low=low)
    ins.update(zip("huv", fields))
    if carried:
        ins.update(sums0=carried[0], square0=carried[1])
    if before:
        ins.update(zip(("prev", "total", "half", "step"), before))
    grad = f32(count, rows, cols)
    outs = dict(sums=f32(3, rows, cols), square=f32(SUB, LANES))
    if not before:
        outs["grad"] = grad
    kinds = (*ins, *outs, *(() if "grad" in outs else ("grad",)))
    result = pl.pallas_call(
        functools.partial(columns_kernel, part[0], cells, kinds),
        name="taper_columns",
        compiler_params=GRANT,
        in_specs=[SMEM if n == "step" else VMEM for n in ins],
        out_specs=[VMEM] * len(outs),
        out_shape=list(outs.values()),
        scratch_shapes=[] if "grad" in outs else [pltpu.VMEM(grad.shape, jnp.float32)],
    )(*ins.values())
    return result[:2], result[2:]


def analysis_kernel(cells, h_ref, u_ref, v_ref, *refs):
    s0_ref, s1_ref, *squares, step_ref = refs[:7]
    *outs, increment_ref = refs[7:]

    @pl.when(pl.program_id(0) == 0)
    def _():
        f0 = factor(0, *squares[:2], step_ref, cells)
        f1 = factor(1, *squares[2:], step_ref, cells)
        increment_ref[...] = f0 * s0_ref[...] - f1 * s1_ref[...]

    begin = pl.program_id(0) * outs[0].shape[0]
    for i, (ref, out) in enumerate(zip((h_ref, u_ref, v_ref), outs)):
        for k in range(outs[0].shape[0]):
            out[k] = ref[begin + k] + increment_ref[i]


def analysis(cells, fields, *rest):
    members, rows, cols = fields[0].shape
    block = pl.BlockSpec((2 * PACK, rows, cols), lambda g: (g, 0, 0))
    return pl.pallas_call(
        functools.partial(analysis_kernel, cells),
        name="analysis",
        compiler_params=GRANT,
        grid=(members // (2 * PACK),),
        in_specs=[VMEM] * 9 + [SMEM],
        out_specs=[block] * 3,
        out_shape=[f32(members, rows, cols)] * 3,
        scratch_shapes=[pltpu.VMEM((3, rows, cols), jnp.float32)],
    )(*fields, *rest)


def parts_of(members):
    sizes, left = [], members // FOLD
    for share in SHARES[:-1]:
        sizes.append(int(round(share * members / FOLD)))
        left -= sizes[-1]
    sizes.append(left)
    begins = np.cumsum([0] + sizes[:-1])
    return [(int(b) * FOLD, n * FOLD) for b, n in zip(begins, sizes) if n]


def per_device(
    height_start, east_start, north_start, obs_value, obs_mask, obs_precision, step_sizes
):
    members, rows, cols = height_start.shape
    starts = (height_start, east_start, north_start)
    top, bottom = pack_rows(*starts)
    above = shifted(bottom, "member", 1, False)
    below = shifted(top, "member", -1, False)
    starts, bottom = lax.optimization_barrier((starts, bottom))
    first, last, *own, east, north, height = pack_columns(*starts)
    hall = shifted(last, "band", 1, True)
    halr = shifted(first, "band", -1, True)
    ends = jnp.concatenate([hall, halr], axis=0)
    cornu = shifted(ends[:, rows - SUB :], "member", 1, False)
    cornd = shifted(ends[:, :SUB], "member", -1, False)

    obs = (obs_value, obs_mask, obs_precision)
    *fields, means = forecast(height, east, north, above, below, *own, hall, halr, cornu, cornd)
    cells = float(members * rows * cols * lax.axis_size("member") * lax.axis_size("band"))
    parts = parts_of(members)

    def sent(slopes):
        return [
            (x, shifted(x, "member", 1, False), shifted(x, "member", -1, False)) for x in slopes
        ]

    def localized(orders, scales, grads):
        heads = [blocks[0] for blocks in orders]
        tapered = []
        for i, part in enumerate(parts):
            blocks = [blocks[i] for blocks in orders]
            x, first, last = taper_rows(part, cells, blocks, heads, scales)
            tapered.append((x, shifted(last, "band", 1, True), shifted(first, "band", -1, True)))
        carried, found = (), []
        for i, (part, arrays) in enumerate(zip(parts, tapered)):
            more = (grads[i], *scales) if grads else ()
            carried, grad = taper_columns(part, cells, *arrays, fields, means, carried, more)
            found += grad
        return *carried, found

    order0 = sent([slopes(part, fields, means, obs) for part in parts])
    sums0, squares0, grads = localized([order0], (), ())
    order1 = sent([slopes(part, fields, means, obs, sums0) for part in parts])
    squares0 = everywhere_sum(squares0)
    sums1, squares1, _ = localized([order0, order1], (*squares0, step_sizes), grads)
    squares1 = everywhere_sum(squares1)
    return tuple(analysis(cells, fields, sums0, sums1, *squares0, *squares1, step_sizes))


def solution(mesh):
    tile, flat = P(None, "member", "band"), P("member", "band")
    return jax.shard_map(
        per_device,
        mesh=mesh,
        in_specs=(tile, tile, tile, flat, flat, flat, P()),
        out_specs=(tile, tile, tile),
        check_vma=False,
    )
```

```python
import functools

import jax
import jax.numpy as jnp
import numpy as np
from jax import lax
from jax.experimental import pallas as pl
from jax.experimental.pallas import tpu as pltpu
from jax.sharding import PartitionSpec as P


STEPS = 3
LWIDTH = 32
LSCALE = 12

LANES = 128
SUB = 8
SLOT = 16
EAST, SIDE = 2 * STEPS, 2 * STEPS - 1
PACK = LANES // SLOT
FOLD = LANES // LWIDTH
SHARES = (0.4, 0.35, 0.25)
DETOURS = (1,)

VMEM = pl.BlockSpec(memory_space=pltpu.VMEM)
SMEM = pl.BlockSpec(memory_space=pltpu.SMEM)
GRANT = pltpu.CompilerParams(vmem_limit_bytes=16 << 20)


def f32(*shape):
    return jax.ShapeDtypeStruct(shape, jnp.float32)


def iota(shape, axis):
    return lax.broadcasted_iota(jnp.int32, shape, axis)


def spin(block, shift, axis):
    shift %= block.shape[axis]
    return block if shift == 0 else pltpu.roll(block, shift, axis)


def swapped(axis, even_side, odd_side, periodic):
    count = lax.axis_size(axis)
    assert count % 2 == 0
    evens = [(i, i + 1) for i in range(0, count, 2)]
    odds = [(i, (i + 1) % count) for i in range(1, count if periodic else count - 1, 2)]
    blocks = []
    for block, pairs in ((even_side, evens), (odd_side, odds)):
        blocks.append(lax.ppermute(block, axis, pairs + [(b, a) for a, b in pairs]))
    return tuple(blocks)


def tile_swaps(block, detour):
    axis = "member"
    count = lax.axis_size(axis)
    if not detour or count < 4 or count % 4:
        return (*swapped(axis, block, block, False), None)
    low, high = count // 2 - 1, count // 2
    evens = [(i, i + 1) for i in range(0, count, 2)]
    odds = [(i, i + 1) for i in range(1, count - 1, 2) if i != low]
    one, two = (
        lax.ppermute(block, axis, pairs + [(b, a) for a, b in pairs])
        for pairs in (evens, odds)
    )
    away = lax.ppermute(block, axis, [(low, count - 1), (high, 0)])
    return one, two, lax.ppermute(away, axis, [(count - 1, high), (0, low)])


def is_even(axis):
    return lax.axis_index(axis) % 2 == 0


def pick(even, first, second):
    return jnp.where(even, second, first), jnp.where(even, first, second)


def everywhere_sum(block):
    half = jnp.zeros_like(block)
    for axis in ("member", "band"):
        count = lax.axis_size(axis)
        if count & (count - 1):
            block, half = lax.psum(block + half, axis), jnp.zeros_like(block)
            continue
        reaches = [1 << k for k in range(count.bit_length() - 1)]
        if axis == "member":
            reaches = reaches[1:] + reaches[:1]
        for reach in reaches:
            block = block + half
            half = lax.ppermute(block, axis, [(i, i ^ reach) for i in range(count)])
    return block, half


def taper(offset):
    scaled = offset.astype(np.float32) / np.float32(LSCALE)
    weight = np.exp(np.float32(-0.5) * scaled * scaled)
    return np.where(np.abs(offset) <= LWIDTH, weight, np.float32(0)).astype(np.float32)


def two_terms(table):
    high = table.astype(jnp.bfloat16)
    low = (table - high.astype(np.float32)).astype(jnp.bfloat16)
    return high, low


def row_table(rows):
    out = np.arange(rows)[:, None]
    table = taper(np.arange(rows + 2 * LWIDTH)[None, :] - LWIDTH - out)
    high, low = two_terms(table)
    return np.block([[high, high], [low, np.zeros_like(low)]])


def column_table(cols):
    out = np.arange(cols)
    high, low = two_terms(taper(out[:, None] - out[None, :]))
    return np.block([[high, low], [high, np.zeros_like(low)]])


def strip_table(cols):
    near = np.arange(LWIDTH)
    left = taper((near - LWIDTH)[:, None] - near[None, :])
    right = taper((cols + near)[:, None] - (cols - LWIDTH + near)[None, :])
    table = np.zeros((2 * LANES, 2 * LANES), np.float32)
    for k in range(FOLD):
        src, dst = k * LWIDTH, 2 * k * LWIDTH
        table[src : src + LWIDTH, dst + LWIDTH : dst + 2 * LWIDTH] = left
        table[LANES + src : LANES + src + LWIDTH, dst : dst + LWIDTH] = right
    return two_terms(table)


def split(block):
    high = block.astype(jnp.bfloat16)
    low = (block - high.astype(jnp.float32)).astype(jnp.bfloat16)
    return high, low


def mm(a, b):
    return jnp.dot(a, b, preferred_element_type=jnp.float32)


SEAM = SLOT // 2


def slot_pack(block, k):
    lane = iota(block.shape, 1) // SLOT
    return jnp.where(lane == k, spin(block, SLOT * k + SEAM, 1), 0.0)


def row_pack_kernel(uf_ref, vf_ref, hf_ref, ul_ref, vl_ref, hl_ref, first_ref, second_ref):
    sub = iota((SUB, LANES), 0)
    even = is_even("member")

    def member(k, _):
        u = uf_ref[k]
        top = (
            jnp.where(sub < 6, vf_ref[k], spin(u, 6, 0)),
            jnp.where(sub < 5, hf_ref[k], spin(u, 3, 0)),
        )
        u = ul_ref[k]
        bottom = (
            jnp.where(sub < 2, spin(u, 5, 0), vl_ref[k]),
            jnp.where(sub < 3, spin(u, 3, 0), hl_ref[k]),
        )
        for i, part in enumerate((slice(0, SUB), slice(SUB, 2 * SUB))):
            second_ref[k, part], first_ref[k, part] = pick(even, bottom[i], top[i])
        return 0

    lax.fori_loop(0, uf_ref.shape[0], member, 0, unroll=4)


def pack_rows(height, eastward, northward):
    members, rows, cols = height.shape
    count = members // 2
    first = pl.BlockSpec((count, SUB, cols), lambda g: (g, 0, 0))
    last = pl.BlockSpec((count, SUB, cols), lambda g: (g, rows // SUB - 1, 0))
    edge = pl.BlockSpec((count, 2 * SUB, cols), lambda g: (g, 0, 0))
    fields = (eastward, northward, height)
    return pl.pallas_call(
        row_pack_kernel,
        name="pack_rows",
        grid=(members // count,),
        in_specs=[first] * 3 + [last] * 3,
        out_specs=[edge] * 2,
        out_shape=[f32(members, 2 * SUB, cols)] * 2,
    )(*fields, *fields)


def column_pack_kernel(u_ref, v_ref, h_ref, first_ref, second_ref, *refs):
    even = is_even("band")
    own_refs, kept_refs = refs[:3], refs[3:]
    members, rows, _ = u_ref.shape
    slot = iota((rows, LANES), 1) % SLOT

    def group(g, _):
        packs = []
        for ref, own, kept in zip((u_ref, v_ref, h_ref), own_refs, kept_refs):
            pack = None
            for k in range(PACK):
                x = ref[g * PACK + k]
                kept[g * PACK + k] = x
                piece = slot_pack(x, k)
                pack = piece if k == 0 else pack + piece
            own[g] = pack
            packs.append(pack)

        def sent(starts):
            u, v, h = (spin(p, at - start, 1) for p, start, at in zip(packs, starts, PLACES))
            return jnp.where(slot < PLACES[1], u, jnp.where(slot < PLACES[2], v, h))

        left = sent((SEAM, SEAM, SEAM))
        right = sent((SEAM - EAST, SEAM - SIDE, SEAM - SIDE))
        second_ref[g], first_ref[g] = pick(even, right, left)
        return 0

    lax.fori_loop(0, members // PACK, group, 0)


PLACES = (0, EAST, EAST + SIDE)


def pack_columns(height, eastward, northward):
    members, rows, cols = height.shape
    groups = members // PACK
    return pl.pallas_call(
        column_pack_kernel,
        name="pack_columns",
        compiler_params=GRANT,
        in_specs=[VMEM] * 3,
        out_specs=[VMEM] * 8,
        out_shape=[f32(groups, rows, LANES)] * 5 + [f32(members, rows, cols)] * 3,
    )(eastward, northward, height)


def corner_kernel(first_ref, second_ref, one_ref, two_ref):
    groups, rows, _ = first_ref.shape
    even_row, even_band = is_even("member"), is_even("band")
    for g in range(groups):
        strips = pick(even_band, first_ref[g], second_ref[g])
        for side, strip in enumerate(strips):
            at = side * groups + g
            two_ref[at], one_ref[at] = pick(even_row, strip[rows - SUB :], strip[:SUB])


def pack_corners(first, second):
    groups = first.shape[0]
    return pl.pallas_call(
        corner_kernel,
        name="pack_corners",
        compiler_params=GRANT,
        in_specs=[VMEM] * 2,
        out_specs=[VMEM] * 2,
        out_shape=[f32(2 * groups, SUB, LANES)] * 2,
    )(first, second)


def difference_table(cols):
    lane = np.arange(cols)
    table = (lane[:, None] == lane[None, :] + 1).astype(np.float32)
    table -= lane[:, None] == lane[None, :] - 1
    return np.concatenate([table, table]).astype(jnp.bfloat16)


def forecast_kernel(
    h_ref, u_ref, v_ref, rowa_ref, rowb_ref, ownu_ref, ownv_ref, ownh_ref, hala_ref, halb_ref,
    corna_ref, cornb_ref, table_ref,
    ho_ref, uo_ref, vo_ref, mean_ref,
    us_ref, vs_ref, hs_ref, lhs_ref, sum_ref,
):
    _, rows, _ = h_ref.shape
    groups = pl.num_programs(0)
    members = groups * PACK
    tall = rows + 2 * SUB
    batch = PACK + 2
    half = batch // 2
    slot = iota((tall, LANES), 1) % SLOT
    row = iota((tall, LANES), 0)
    sub = iota((SUB, LANES), 0)
    here, tiles = lax.axis_index("member"), lax.axis_size("member")
    even_row, even_band = is_even("member"), is_even("band")
    outside = ((row < SUB) & (here == 0)) | ((row >= rows + SUB) & (here == tiles - 1))
    pull = jnp.where(outside, 0.0, 0.2)
    mid, low, high = slice(SUB, SUB + tall), slice(SUB - 1, SUB + tall - 1), slice(SUB + 1, SUB + tall + 1)
    core = slice(2 * SUB, 2 * SUB + rows)

    ends = (iota((tall, LANES), 1) == 0) | (iota((tall, LANES), 1) == LANES - 1)
    order = (PACK, PACK + 1, *range(PACK))

    def differences(ref):
        right = spin(ref[PACK + 1, mid], -2, 1)
        wall = jnp.where(slot == SEAM - 1, -ref[PACK, mid], right)
        for start in (0, half):
            for at, j in enumerate(order[start : start + half], start):
                for i, part in enumerate(split(ref[j, mid])):
                    lhs_ref[at, :, i * LANES : (i + 1) * LANES] = part
            stack = lhs_ref[start : start + half].reshape(half * tall, 2 * LANES)
            d = mm(stack, table_ref[...])
            for at, j in enumerate(order[start : start + half]):
                piece = d[at * tall : (at + 1) * tall]
                if j < PACK:
                    piece += jnp.where(ends, spin(wall, -(SLOT * j + SEAM - 1), 1), 0.0)
                yield j, piece

    def group():
        packs = [[None] * 2 for _ in range(3)]
        for k in range(PACK):
            m = k
            a0, b0 = pick(even_row, rowa_ref[m, :SUB], rowb_ref[m, :SUB])
            a1, b1 = pick(even_row, rowa_ref[m, SUB:], rowb_ref[m, SUB:])
            ua = jnp.where(sub < 5, spin(a0, 3, 0), spin(a1, 5, 0))
            ub = jnp.where(sub < 2, spin(b0, 2, 0), spin(b1, 5, 0))
            ends = ((us_ref, ua, ub, u_ref), (vs_ref, a0, b0, v_ref), (hs_ref, a1, b1, h_ref))
            for i, (state, a, b, ref) in enumerate(ends):
                state[k, SUB : 2 * SUB] = a
                state[k, core] = ref[m]
                state[k, 2 * SUB + rows : 3 * SUB + rows] = b
                for end, edge in enumerate((a, b)):
                    piece = slot_pack(edge, k)
                    packs[i][end] = piece if k == 0 else packs[i][end] + piece
        strips = []
        for side, strip in enumerate(pick(even_band, hala_ref[0], halb_ref[0])):
            over, under = pick(even_row, corna_ref[side, 0], cornb_ref[side, 0])
            strips.append(jnp.concatenate([over, strip, under], axis=0))
        left, right = strips
        owns = ((us_ref, ownu_ref, EAST), (vs_ref, ownv_ref, SIDE), (hs_ref, ownh_ref, SIDE))
        for i, (state, own_ref, size) in enumerate(owns):
            own = jnp.concatenate([packs[i][0], own_ref[0], packs[i][1]], axis=0)
            state[PACK, mid] = jnp.where(slot < SEAM, spin(left, SEAM - size - PLACES[i], 1), own)
            state[PACK + 1, mid] = jnp.where(slot < SEAM, own, spin(right, SEAM - PLACES[i], 1))

        for step in range(STEPS):
            last = step == STEPS - 1
            for j, d in differences(us_ref):
                hs_ref[j, mid] = hs_ref[j, mid] - pull * (d + (vs_ref[j, high] - vs_ref[j, low]))
            for j, d in differences(hs_ref):
                if last and j >= PACK:
                    continue
                u, v = us_ref[j, mid], vs_ref[j, mid]
                us_ref[j, mid] = u + 0.1 * v - pull * d
                vs_ref[j, mid] = v - 0.1 * u - pull * (hs_ref[j, high] - hs_ref[j, low])

        for i, (state, out) in enumerate(((hs_ref, ho_ref), (us_ref, uo_ref), (vs_ref, vo_ref))):
            total = sum_ref[i]
            for k in range(PACK):
                x = state[k, core]
                out[k] = x
                total = total + x
            sum_ref[i] = total

    @pl.when(pl.program_id(0) == 0)
    def _():
        sum_ref[...] = jnp.zeros_like(sum_ref)
        for state in (us_ref, vs_ref, hs_ref):
            for j in range(batch):
                state[j, :SUB] = jnp.zeros((SUB, LANES), jnp.float32)
                state[j, SUB + tall :] = jnp.zeros((SUB, LANES), jnp.float32)

    group()

    @pl.when(pl.program_id(0) == groups - 1)
    def _():
        for i in range(3):
            mean_ref[i] = sum_ref[i] * (1.0 / members)


def forecast(h, u, v, rowa, rowb, *rest):
    members, rows, cols = h.shape
    groups = members // PACK
    tall = rows + 2 * SUB
    state = pltpu.VMEM((PACK + 2, tall + 2 * SUB, LANES), jnp.float32)
    *strips, corna, cornb = rest
    corna, cornb = (x.reshape(2, groups, SUB, LANES) for x in (corna, cornb))
    tile = pl.BlockSpec((PACK, rows, cols), lambda g: (g, 0, 0))
    side = pl.BlockSpec((PACK, 2 * SUB, cols), lambda g: (g, 0, 0))
    strip = pl.BlockSpec((1, rows, LANES), lambda g: (g, 0, 0))
    corner = pl.BlockSpec((2, 1, SUB, LANES), lambda g: (0, g, 0, 0))
    mean = pl.BlockSpec((3, rows, cols), lambda g: (0, 0, 0))
    return pl.pallas_call(
        forecast_kernel,
        name="forecast",
        compiler_params=GRANT,
        grid=(groups,),
        in_specs=[tile] * 3 + [side] * 2 + [strip] * 5 + [corner] * 2 + [VMEM],
        out_specs=[tile] * 3 + [mean],
        out_shape=[f32(members, rows, cols)] * 3 + [f32(3, rows, cols)],
        scratch_shapes=[
            state,
            state,
            state,
            pltpu.VMEM((PACK + 2, tall, 2 * LANES), jnp.bfloat16),
            pltpu.VMEM((3, rows, cols), jnp.float32),
        ],
    )(h, u, v, rowa, rowb, *strips, corna, cornb, difference_table(cols))


def factor(k, square_ref, half_ref, step_ref, cells):
    total = jnp.sum(square_ref[...] + half_ref[...], keepdims=True)
    return step_ref[k].astype(jnp.float32) / 64.0 / jnp.sqrt(total / cells + 1e-06)


def slope_kernel(begin, h_ref, u_ref, v_ref, mean_ref, value_ref, seen_ref, precise_ref, *refs):
    *sums, out_ref = refs
    members = h_ref.shape[0]
    extra = 2 if sums else 1
    count = out_ref.shape[0] - (0 if begin else extra)
    scale = 1.0 / float(np.sqrt(np.float32(members - 1)))
    mh, mu, mv = (mean_ref[i] for i in range(3))
    value, weight = value_ref[...], seen_ref[...].astype(jnp.float32) * precise_ref[...]
    if sums:
        dh, du, dv = (sums[0][i] for i in range(3))
        eu, ev = (0.3 * scale) * du, (0.3 * scale) * dv
        rests = (
            -weight * (dh + 0.3 * (mu * du + mv * dv)),
            (-0.15 * weight) * (du * du + dv * dv),
        )
    else:
        eu, ev = (0.3 * scale) * mu, (0.3 * scale) * mv
        rests = (weight * (value - mh - 0.15 * (mu * mu + mv * mv)),)
    if not begin:
        for i, rest in enumerate(rests):
            out_ref[count + i] = rest

    def member(m, _):
        slope = eu * (u_ref[begin + m] - mu) + ev * (v_ref[begin + m] - mv)
        if not sums:
            slope = (h_ref[begin + m] - mh) * scale + slope
        out_ref[m] = slope
        return 0

    lax.fori_loop(0, count, member, 0, unroll=4)


def slopes(part, fields, means, obs, *sums):
    begin, count = part
    extra = 0 if begin else 1 + len(sums)
    return pl.pallas_call(
        functools.partial(slope_kernel, begin),
        name="slopes",
        compiler_params=GRANT,
        in_specs=[VMEM] * (7 + len(sums)),
        out_specs=VMEM,
        out_shape=f32(count + extra, *fields[0].shape[1:]),
    )(*fields, means, *obs, *sums)


def rows_kernel(cells, sizes, shared, *refs):
    orders = len(sizes)
    blocks = []
    for size in sizes:
        blocks.append(refs[:size])
        refs = refs[size:]
    heads = [refs[3 * i : 3 * i + 3] for i in range(orders)] if shared else blocks
    refs = refs[3 * orders * shared :]
    *scales, table_ref, out_ref, first_ref, second_ref = refs
    members, rows, cols = out_ref.shape
    rest_at = heads[0][0].shape[0] - 1
    lane = iota((rows, LANES), 1)
    table = table_ref[...]

    even_row, even_band = is_even("member"), is_even("band")

    def tall(trio, m):
        own, one, two, *came = trio
        above, below = pick(even_row, one[m], two[m])
        if came:
            here, tiles = lax.axis_index("member"), lax.axis_size("member")
            above = jnp.where(here == tiles // 2, came[0][m], above)
            below = jnp.where(here == tiles // 2 - 1, came[0][m], below)
        return jnp.concatenate([above, own[m], below], axis=0)

    rest = tall(heads[0], rest_at)
    if orders > 1:
        f = factor(0, *scales, cells)
        rest = rest + f * (tall(heads[1], rest_at) + f * tall(heads[1], rest_at + 1))

    def fold(g, _):
        left = right = None
        for pair in range(FOLD // 2):
            halves = []
            for k in (2 * pair, 2 * pair + 1):
                m = g * FOLD + k
                slope = tall(blocks[0], m)
                if orders > 1:
                    slope = slope + f * tall(blocks[1], m)
                high, low = split(slope * rest)
                halves.append(jnp.concatenate([high, low], axis=0))
            both = mm(table, jnp.concatenate(halves, axis=1))
            both = both[:rows] + both[rows:]
            for k in (2 * pair, 2 * pair + 1):
                y = both[:, (k % 2) * cols : (k % 2 + 1) * cols]
                out_ref[g * FOLD + k] = y
                here = lane // LWIDTH == k
                l = jnp.where(here, spin(y, LWIDTH * k, 1), 0.0)
                r = jnp.where(here, spin(y, LWIDTH * k + LWIDTH - cols, 1), 0.0)
                left, right = (l, r) if k == 0 else (left + l, right + r)
        second_ref[g], first_ref[g] = pick(even_band, right, left)
        return 0

    lax.fori_loop(0, members // FOLD, fold, 0, unroll=2)


def taper_rows(part, cells, blocks, heads, scales):
    begin, members = part
    _, rows, cols = blocks[0][0].shape
    folds = members // FOLD
    shared = bool(begin)
    sizes = [len(block) for block in blocks]
    arrays = [x for block in blocks + (heads if shared else []) for x in block]
    return pl.pallas_call(
        functools.partial(rows_kernel, cells, sizes, shared),
        name="taper_rows",
        compiler_params=GRANT,
        in_specs=[VMEM] * len(arrays) + ([VMEM, VMEM, SMEM] if scales else []) + [VMEM],
        out_specs=[VMEM] * 3,
        out_shape=[f32(members, rows, cols)] + [f32(folds, rows, LANES)] * 2,
    )(*arrays, *scales, row_table(rows))


def columns_kernel(begin, cells, kinds, *refs):
    names = dict(zip(kinds, refs))
    x_ref, one_ref, two_ref = (names[n] for n in ("x", "one", "two"))
    even = is_even("band")
    mean_ref, sums_ref, square_ref = (names[n] for n in ("means", "sums", "square"))
    grad_ref = names["grad"]
    fields = [names[n] for n in "huv"]
    count, rows, cols = x_ref.shape
    scale = 1.0 / float(np.sqrt(np.float32(fields[0].shape[0] - 1)))
    lane = iota((rows, LANES), 1)
    rim = (lane < LWIDTH) | (lane >= cols - LWIDTH)

    def fold(g, _):
        xh, xl = split(jnp.concatenate(pick(even, one_ref[g], two_ref[g]), axis=1))
        high_table = names["high"][...]
        strips = mm(xh, high_table) + (mm(xl, high_table) + mm(xh, names["low"][...]))
        block = jnp.concatenate([x_ref[g * FOLD + k] for k in range(FOLD)], axis=0)
        bh, bl = split(block)
        both = mm(jnp.concatenate([bh, bl], axis=1), names["table"][...])
        both = both[:, :cols] + both[:, cols:]
        for k in range(FOLD):
            at = 2 * k * LWIDTH
            part = strips[:, at // LANES * LANES : at // LANES * LANES + LANES]
            part = spin(part, -(at % LANES + LWIDTH), 1)
            y = both[k * rows : (k + 1) * rows] + jnp.where(rim, part, 0.0)
            grad_ref[g * FOLD + k] = y
        return 0

    lax.fori_loop(0, count // FOLD, fold, 0, unroll=2)
    zero = jnp.zeros((SUB, cols), jnp.float32)
    square = names["square0"][...] if "square0" in names else zero
    if "prev" in names:
        f = factor(0, names["total"], names["half"], names["step"], cells)
    for start in range(0, rows, SUB):
        part = slice(start, start + SUB)
        means = [mean_ref[i, part] for i in range(3)]

        def member(m, carry):
            square, *sums = carry
            y = grad_ref[m, part]
            if "prev" in names:
                y = f * names["prev"][m, part] - y
            square = square + y * y
            terms = ((ref[begin + m, part] - mean) * y for ref, mean in zip(fields, means))
            return (square, *(s + t for s, t in zip(sums, terms)))

        square, *sums = lax.fori_loop(0, count, member, (square, zero, zero, zero), unroll=8)
        for i in range(3):
            total = sums[i] * scale
            if "sums0" in names:
                total = total + names["sums0"][i, part]
            sums_ref[i, part] = total
    square_ref[...] = square


def taper_columns(part, cells, x, one, two, fields, means, carried, before):
    count, rows, cols = x.shape
    high, low = strip_table(cols)
    ins = dict(x=x, one=one, two=two, means=means, table=column_table(cols), high=high, low=low)
    ins.update(zip("huv", fields))
    if carried:
        ins.update(sums0=carried[0], square0=carried[1])
    if before:
        ins.update(zip(("prev", "total", "half", "step"), before))
    grad = f32(count, rows, cols)
    outs = dict(sums=f32(3, rows, cols), square=f32(SUB, LANES))
    if not before:
        outs["grad"] = grad
    kinds = (*ins, *outs, *(() if "grad" in outs else ("grad",)))
    result = pl.pallas_call(
        functools.partial(columns_kernel, part[0], cells, kinds),
        name="taper_columns",
        compiler_params=GRANT,
        in_specs=[SMEM if n == "step" else VMEM for n in ins],
        out_specs=[VMEM] * len(outs),
        out_shape=list(outs.values()),
        scratch_shapes=[] if "grad" in outs else [pltpu.VMEM(grad.shape, jnp.float32)],
    )(*ins.values())
    return result[:2], result[2:]


def analysis_kernel(cells, h_ref, u_ref, v_ref, *refs):
    s0_ref, s1_ref, *squares, step_ref = refs[:7]
    *outs, increment_ref = refs[7:]

    @pl.when(pl.program_id(0) == 0)
    def _():
        f0 = factor(0, *squares[:2], step_ref, cells)
        f1 = factor(1, *squares[2:], step_ref, cells)
        increment_ref[...] = f0 * s0_ref[...] - f1 * s1_ref[...]

    begin = pl.program_id(0) * outs[0].shape[0]
    for i, (ref, out) in enumerate(zip((h_ref, u_ref, v_ref), outs)):
        for k in range(outs[0].shape[0]):
            out[k] = ref[begin + k] + increment_ref[i]


def analysis(cells, fields, *rest):
    members, rows, cols = fields[0].shape
    block = pl.BlockSpec((2 * PACK, rows, cols), lambda g: (g, 0, 0))
    return pl.pallas_call(
        functools.partial(analysis_kernel, cells),
        name="analysis",
        compiler_params=GRANT,
        grid=(members // (2 * PACK),),
        in_specs=[VMEM] * 9 + [SMEM],
        out_specs=[block] * 3,
        out_shape=[f32(members, rows, cols)] * 3,
        scratch_shapes=[pltpu.VMEM((3, rows, cols), jnp.float32)],
    )(*fields, *rest)


def parts_of(members):
    sizes, left = [], members // FOLD
    for share in SHARES[:-1]:
        sizes.append(int(round(share * members / FOLD)))
        left -= sizes[-1]
    sizes.append(left)
    begins = np.cumsum([0] + sizes[:-1])
    return [(int(b) * FOLD, n * FOLD) for b, n in zip(begins, sizes) if n]


def per_device(
    height_start, east_start, north_start, obs_value, obs_mask, obs_precision, step_sizes
):
    members, rows, cols = height_start.shape
    starts = (height_start, east_start, north_start)
    first, second = pack_rows(*starts)
    rows_swaps = swapped("member", first, second, False)
    starts, first = lax.optimization_barrier((starts, first))
    first, second, *own, east, north, height = pack_columns(*starts)
    band_swaps = swapped("band", first, second, True)
    corners = swapped("member", *pack_corners(*band_swaps), False)

    obs = (obs_value, obs_mask, obs_precision)
    *fields, means = forecast(height, east, north, *rows_swaps, *own, *band_swaps, *corners)
    cells = float(members * rows * cols * lax.axis_size("member") * lax.axis_size("band"))
    parts = parts_of(members)

    def sent(slopes):
        blocks = []
        for i, x in enumerate(slopes):
            one, two, came = tile_swaps(x, i in DETOURS)
            blocks.append((x, one, two) if came is None else (x, one, two, came))
        return blocks

    def localized(orders, scales, grads):
        heads = [blocks[0] for blocks in orders]
        tapered = []
        for i, part in enumerate(parts):
            blocks = [blocks[i] for blocks in orders]
            x, first, last = taper_rows(part, cells, blocks, heads, scales)
            tapered.append((x, *swapped("band", first, last, True)))
        carried, found = (), []
        for i, (part, arrays) in enumerate(zip(parts, tapered)):
            more = (grads[i], *scales) if grads else ()
            carried, grad = taper_columns(part, cells, *arrays, fields, means, carried, more)
            found += grad
        return *carried, found

    order0 = sent([slopes(part, fields, means, obs) for part in parts])
    sums0, squares0, grads = localized([order0], (), ())
    order1 = sent([slopes(part, fields, means, obs, sums0) for part in parts])
    squares0 = everywhere_sum(squares0)
    sums1, squares1, _ = localized([order0, order1], (*squares0, step_sizes), grads)
    squares1 = everywhere_sum(squares1)
    return tuple(analysis(cells, fields, sums0, sums1, *squares0, *squares1, step_sizes))


def solution(mesh):
    tile, flat = P(None, "member", "band"), P("member", "band")

    return jax.shard_map(
        per_device,
        mesh=mesh,
        in_specs=(tile, tile, tile, flat, flat, flat, P()),
        out_specs=(tile, tile, tile),
        check_vma=False,
    )
```
